32 devices in a mesh: groups: 2 (over x), cluster: 16 (over z, y, core).
Axes of the slice: x: 2, y: 2, z: 4, core: 2. Of those that a mesh axis runs over, the one named last changes fastest.
Arguments:
- hidden_states: bfloat16 [128, 128, 1024], P(('groups', 'cluster')), parts along dimension 0, may hold values from -6 to 6
- token_ids: int32 [128, 128], P(('groups', 'cluster')), parts along dimension 0, may hold values from 0 to 30521, as said below
- up_weight: bfloat16 [1024, 2048], replicated, may hold values from -0.1875 to 0.1875
- down_weight: bfloat16 [2048, 1024], replicated, may hold values from -0.125 to 0.125
- centroids: bfloat16 [65536, 1024], P('cluster'), may hold values from -0.1875 to 0.1875
- positives: int32 [128, 16], P('groups'), parts along dimension 0, may hold values from 0 to 65535
- counts: int32 [128], P('groups'), parts along dimension 0, may hold values from 1 to 16
Outputs:
- query_grad: float32 [128, 1024], P(('groups', 'cluster')), parts along dimension 0
- centroid_grad: float32 [131072, 1024], P(('groups', 'cluster')), parts along dimension 0
The draws below stay inside these ranges and needn't reach their ends.
There are 2 independent parts, one for each index of `groups`. The reference program is written for one: setup_inputs(seed, part) draws one part's arguments, and reference() takes and returns one part's arrays. A program takes and returns all parts, laid end to end along the dimension named above; an argument that names none is the same for every part. Nothing has to cross between parts.
Inputs may be any that keep to these rules, and one draw needn't show every extreme that they name: `token_ids`: in each query's row the nonzero ids come first and zeros fill the rest; every query has at least 16 nonzero ids.
All inputs are finite; a program needn't handle non-finite values.
Results may differ from the reference program's by a relative error of at most 0.003.
Values may be sent and summed in bfloat16 or wider, within the bound.
No kernel may reach another device: no remote copies, remote signals or barrier semaphores. Data moves between devices by JAX's collectives and lax.ppermute only.
A program may use at most 128 MiB of HBM per device.

```python
import jax
import jax.numpy as jnp
from jax import lax

D = 1024
FF = 2048
SEQ = 128
CLUSTERS = 65536
VOCAB = 30522
POS = 16
MB = 32
QUERIES = 64
N_CLUSTER = 16


def draw_token_ids(key, part):
    first_key, second_key = jax.random.split(jax.random.fold_in(key, 11))
    lengths = jax.random.randint(first_key, (QUERIES,), SEQ // 8, SEQ + 1)
    lengths = lengths.at[0].set(SEQ // 8)
    values = jax.random.randint(second_key, (QUERIES, SEQ), 1, VOCAB)
    values = values.at[0, 0].set(VOCAB - 1)
    places = jnp.arange(SEQ, dtype=jnp.int32)
    return jnp.where(places[None, :] < lengths[:, None], values, 0).astype(jnp.int32)


def set_ends(values, key, low, high):
    longest = values.shape.index(max(values.shape))
    spots = []
    for shift in (0, 1):
        where = [jax.random.randint(jax.random.fold_in(key, axis), (), 0, length) for axis, length in enumerate(values.shape)]
        where[longest] = (where[longest] + shift) % values.shape[longest]
        spots.append(tuple(where))
    return values.at[spots[0]].set(low).at[spots[1]].set(high)


def shard_levels(key, extent, shards, low, high):
    def one(dim, shards_of):
        steps = jax.random.uniform(jax.random.fold_in(jax.random.fold_in(key, 6), dim), (shards_of,), jnp.float32, low / len(shards), high / len(shards))
        return jnp.repeat(jnp.exp(steps), extent[dim] // shards_of).reshape((-1,) + (1,) * (len(extent) - dim - 1))

    factor_of = one(*shards[0])
    for cut in shards[1:]:
        factor_of = factor_of * one(*cut)
    return factor_of


def normal_values(own_key, dims, scale, most, cuts=(), kind=jnp.bfloat16):
    gain = shard_levels(own_key, dims, cuts, -0.22, 0.18) if cuts else 1.0
    drawn = jax.random.normal(own_key, dims, jnp.float32) * scale * gain
    return jnp.minimum(jnp.maximum(drawn, -most), most).astype(kind)


def setup_inputs(seed: int = 0, part: int = 0) -> dict:
    splits = jax.random.split(jax.random.key(seed), 8)
    own_keys = jax.random.split(jax.random.fold_in(splits[7], part), 8)
    return {
        "hidden_states": normal_values(own_keys[0], (QUERIES, SEQ, D), 1.0, 6.0, ((0, 16),)),
        "token_ids": draw_token_ids(jax.random.fold_in(jax.random.fold_in(splits[7], part), 71), part),
        "up_weight": normal_values(splits[2], (D, FF), D ** -0.5, 0.1875),
        "down_weight": normal_values(splits[3], (FF, D), FF ** -0.5, 0.125),
        "centroids": normal_values(splits[4], (CLUSTERS, D), D ** -0.5, 0.1875, ((0, 16),)),
        "positives": set_ends(jax.random.randint(own_keys[5], (QUERIES, POS), 0, CLUSTERS), jax.random.fold_in(own_keys[5], 1), 0, CLUSTERS - 1).astype(jnp.int32),
        "counts": set_ends(jax.random.randint(own_keys[6], (QUERIES,), 1, POS + 1), jax.random.fold_in(own_keys[6], 1), 1, POS).astype(jnp.int32),
    }


def layer_norm(values):
    centered = values - lax.optimization_barrier(jnp.mean(values, axis=-1, keepdims=True))
    spread = lax.optimization_barrier(jnp.mean(centered * centered, axis=-1, keepdims=True))
    return centered * lax.rsqrt(spread + 1e-05)

def encode(states, ids, up_weight, down_weight):
    count = states.shape[0]
    flat = states.reshape(count * SEQ, D)
    up_part = jnp.dot(flat, up_weight, preferred_element_type=jnp.float32)
    act = jax.nn.gelu(up_part).astype(jnp.bfloat16)
    ffn = jnp.dot(act, down_weight, preferred_element_type=jnp.float32)
    normed = layer_norm(flat.astype(jnp.float32) + ffn).reshape(count, SEQ, D)
    keep = (ids != 0).astype(jnp.float32)
    pooled = lax.optimization_barrier(jnp.sum(normed * keep[:, :, None], axis=1)) / lax.optimization_barrier(jnp.sum(keep, axis=1))[:, None]
    return layer_norm(pooled).astype(jnp.bfloat16)

def reference(hidden_states, token_ids, up_weight, down_weight, centroids, positives, counts):
    q_dev = QUERIES // N_CLUSTER
    c_dev = CLUSTERS // N_CLUSTER
    grouped = hidden_states.reshape(N_CLUSTER, q_dev, SEQ, D)
    grouped_ids = token_ids.reshape(N_CLUSTER, q_dev, SEQ)
    queries = lax.map(lambda pair: encode(pair[0], pair[1], up_weight, down_weight), (grouped, grouped_ids))
    queries = queries.reshape(QUERIES, D)
    valid = jnp.arange(POS, dtype=jnp.int32)[None, :] < counts[:, None]

    def score(total, block):
        cent_block, start = block
        logits = jnp.dot(queries, cent_block.T, preferred_element_type=jnp.float32)
        cluster_ids = start + jnp.arange(c_dev, dtype=jnp.int32)
        hits = (positives[:, :, None] == cluster_ids[None, None, :]) & valid[:, :, None]
        target = jnp.any(hits, axis=1).astype(jnp.float32)
        dlogit = ((jax.nn.sigmoid(logits) - target) / MB).astype(jnp.bfloat16)
        total = total + jnp.dot(dlogit, cent_block, preferred_element_type=jnp.float32)
        cent_grad = jnp.dot(dlogit.T, queries, preferred_element_type=jnp.float32)
        return (total, cent_grad)
    starts = jnp.arange(N_CLUSTER, dtype=jnp.int32) * c_dev
    blocks = centroids.reshape(N_CLUSTER, c_dev, D)
    query_grad, cent_grads = lax.scan(score, jnp.zeros((QUERIES, D), jnp.float32), (blocks, starts))
    return (query_grad, cent_grads.reshape(CLUSTERS, D))
```

```python
import functools

import jax
import jax.numpy as jnp
from jax import lax
from jax.experimental import pallas as pl
from jax.experimental.pallas import tpu as pltpu
from jax.sharding import PartitionSpec as P

MB = 32
EPS = 1e-05
F32 = jnp.float32
BF16 = jnp.bfloat16
HBM = pltpu.MemorySpace.HBM
NN = (((1,), (0,)), ((), ()))
NT = (((1,), (1,)), ((), ()))
TN = (((0,), (0,)), ((), ()))


def dot(a, b, dims):
    return lax.dot_general(a, b, dims, preferred_element_type=F32)


def whole(shape):
    return pl.BlockSpec(shape, lambda: (0,) * len(shape))


def normed(values):
    centered = values - jnp.mean(values, axis=-1, keepdims=True)
    spread = jnp.mean(centered * centered, axis=-1, keepdims=True)
    return centered, lax.rsqrt(spread + EPS)


def encode_kernel(up_step, down_step, x_hbm, ids_ref, up_hbm, down_hbm, q_ref, x_ref, up_ref, down_ref, act_ref, sum_ref, sems):
    count, length, width = x_ref.shape
    hidden = up_ref.shape[1]
    x_copy = pltpu.make_async_copy(x_hbm, x_ref, sems.at[0, 0])
    x_copy.start()
    ups, downs = [], []
    for k in range(hidden // up_step):
        cut = (slice(None), pl.ds(k * up_step, up_step))
        ups.append(pltpu.make_async_copy(up_hbm.at[cut], up_ref.at[cut], sems.at[1, k]))
    for k in range(width // down_step):
        cut = (slice(None), pl.ds(k * down_step, down_step))
        downs.append(pltpu.make_async_copy(down_hbm.at[cut], down_ref.at[cut], sems.at[2, k]))
    for copy in ups + downs:
        copy.start()
    x_copy.wait()
    x = x_ref[...].reshape(count * length, width)
    for k, copy in enumerate(ups):
        copy.wait()
        cut = slice(k * up_step, (k + 1) * up_step)
        act_ref[:, cut] = jax.nn.gelu(dot(x, up_ref[:, cut], NN)).astype(BF16)
    for k, copy in enumerate(downs):
        copy.wait()
        cut = slice(k * down_step, (k + 1) * down_step)
        sum_ref[:, cut] = x[:, cut].astype(F32) + dot(act_ref[...], down_ref[:, cut], NN)
    kept = jnp.sum((ids_ref[...] != 0).astype(F32), axis=1, keepdims=True)
    place = lax.broadcasted_iota(jnp.int32, (length, 1), 0).astype(F32)
    rows = []
    for k in range(count):
        centered, scale = normed(sum_ref[k * length : (k + 1) * length, :])
        own = kept[k : k + 1, :]
        scale = jnp.where(place < own, scale, 0.0)
        rows.append(jnp.sum(centered * scale, axis=0, keepdims=True) / own)
    centered, scale = normed(jnp.concatenate(rows, axis=0))
    q_ref[0] = (centered * scale).astype(BF16)


def encode(states, ids, up_weight, down_weight):
    count, length, width = states.shape
    hidden = up_weight.shape[1]
    up_step, down_step = min(512, hidden), min(256, width)
    steps = max(hidden // up_step, width // down_step)
    tokens = count * length
    return pl.pallas_call(
        functools.partial(encode_kernel, up_step, down_step),
        out_shape=jax.ShapeDtypeStruct((1, count, width), BF16),
        in_specs=[
            pl.BlockSpec(memory_space=HBM),
            whole(ids.shape),
            pl.BlockSpec(memory_space=HBM),
            pl.BlockSpec(memory_space=HBM),
        ],
        out_specs=whole((1, count, width)),
        scratch_shapes=[
            pltpu.VMEM(states.shape, BF16),
            pltpu.VMEM(up_weight.shape, BF16),
            pltpu.VMEM(down_weight.shape, BF16),
            pltpu.VMEM((tokens, hidden), BF16),
            pltpu.VMEM((tokens, width), F32),
            pltpu.SemaphoreType.DMA((3, steps)),
        ],
        compiler_params=pltpu.CompilerParams(vmem_limit_bytes=60 << 20),
        cost_estimate=pl.CostEstimate(
            flops=4 * tokens * hidden * width,
            transcendentals=tokens * hidden,
            bytes_accessed=4 * hidden * width + 2 * tokens * width,
        ),
        name="encode",
    )(states, ids, up_weight, down_weight)


def target_kernel(order, me_ref, pos_ref, cnt_ref, out_ref, rel_ref):
    slots, queries = pos_ref.shape
    c_dev = out_ref.shape[1]
    per = rel_ref.shape[1]
    me = me_ref[0]
    slot = lax.broadcasted_iota(jnp.int32, (slots, queries), 0)
    rel = jnp.where(slot < cnt_ref[...], pos_ref[...] - me * c_dev, -1).T
    for k in range(queries // per):
        rel_ref[k] = rel[k * per : (k + 1) * per, :]
    rel = jnp.concatenate([rel_ref[lax.bitwise_xor(me, k)] for k in order], axis=0)
    step = min(512, c_dev)
    for k in range(c_dev // step):
        ids = lax.broadcasted_iota(jnp.int32, (queries, step), 1) + k * step
        hit = ids == rel[:, 0:1]
        for s in range(1, slots):
            hit = jnp.logical_or(hit, ids == rel[:, s : s + 1])
        out_ref[:, k * step : (k + 1) * step] = jnp.where(hit, 1.0 / MB, 0.0)


def targets(me, positives, counts, order, c_dev):
    queries, slots = positives.shape
    return pl.pallas_call(
        functools.partial(target_kernel, order),
        out_shape=jax.ShapeDtypeStruct((queries, c_dev), F32),
        in_specs=[
            pl.BlockSpec(memory_space=pltpu.SMEM),
            whole((slots, queries)),
            whole((1, queries)),
        ],
        out_specs=whole((queries, c_dev)),
        scratch_shapes=[pltpu.VMEM((len(order), queries // len(order), slots), jnp.int32)],
        compiler_params=pltpu.CompilerParams(vmem_limit_bytes=8 << 20),
        cost_estimate=pl.CostEstimate(
            flops=2 * queries * slots * c_dev, transcendentals=0, bytes_accessed=4 * queries * c_dev
        ),
        name="targets",
    )(me.reshape(1), positives.T, counts.reshape(1, queries))


def score_kernel(c_ref, q_ref, target_ref, keep_ref, send_ref, dlogit_ref):
    c_dev = c_ref.shape[0]
    half = keep_ref.shape[0]
    step = min(512, c_dev)
    queries = q_ref[...]
    for k in range(c_dev // step):
        cut = slice(k * step, (k + 1) * step)
        logits = dot(c_ref[cut, :], queries, NT).T
        dlogit_ref[:, cut] = (jax.nn.sigmoid(logits) * (1.0 / MB) - target_ref[:, cut]).astype(BF16)
    grad = dot(dlogit_ref[...], c_ref[...], NN)
    keep_ref[...] = grad[:half]
    send_ref[...] = grad[half:]


def score(centroids, queries, target):
    c_dev, width = centroids.shape
    count = queries.shape[0]
    half = count // 2
    return pl.pallas_call(
        score_kernel,
        out_shape=(
            jax.ShapeDtypeStruct((half, width), F32),
            jax.ShapeDtypeStruct((half, width), F32),
            jax.ShapeDtypeStruct((count, c_dev), BF16),
        ),
        in_specs=[whole((c_dev, width)), whole((count, width)), whole((count, c_dev))],
        out_specs=(whole((half, width)), whole((half, width)), whole((count, c_dev))),
        compiler_params=pltpu.CompilerParams(vmem_limit_bytes=32 << 20),
        cost_estimate=pl.CostEstimate(
            flops=4 * count * c_dev * width, transcendentals=count * c_dev, bytes_accessed=2 * c_dev * width
        ),
        name="score",
    )(centroids, queries, target)


def outer_kernel(first, sub, dlogit_ref, q_ref, *rest):
    out_hbm, held_ref, sems = rest[-3:]
    queries = q_ref[...]
    copies = []
    for k in range(held_ref.shape[0] // sub):
        cut = slice(k * sub, (k + 1) * sub)
        held_ref[cut, :] = dot(dlogit_ref[:, cut], queries, TN)
        copies.append(
            pltpu.make_async_copy(held_ref.at[cut], out_hbm.at[pl.ds(first + k * sub, sub)], sems.at[k])
        )
        copies[-1].start()
    for copy in copies:
        copy.wait()


def outer(dlogit, queries, piece, pieces, grown):
    count, c_dev = dlogit.shape
    width = queries.shape[1]
    rows = c_dev // pieces
    sub = min(256, rows)
    return pl.pallas_call(
        functools.partial(outer_kernel, piece * rows, sub),
        out_shape=jax.ShapeDtypeStruct((c_dev, width), F32),
        grid=(1,),
        in_specs=[
            pl.BlockSpec((count, rows), lambda i: (0, piece)),
            pl.BlockSpec((count, width), lambda i: (0, 0)),
        ]
        + [pl.BlockSpec(memory_space=HBM)] * len(grown),
        out_specs=pl.BlockSpec(memory_space=HBM),
        scratch_shapes=[pltpu.VMEM((rows, width), F32), pltpu.SemaphoreType.DMA((rows // sub,))],
        input_output_aliases={2: 0} if grown else {},
        compiler_params=pltpu.CompilerParams(vmem_limit_bytes=16 << 20),
        cost_estimate=pl.CostEstimate(
            flops=2 * count * rows * width, transcendentals=0, bytes_accessed=4 * rows * width
        ),
        name="outer",
    )(dlogit, queries, *grown)


def shards(n, hidden_states, token_ids, up_weight, down_weight, centroids, positives, counts):
    me = lax.axis_index("cluster")
    bits = n.bit_length() - 1
    order = [int(format(k, f"0{bits}b")[::-1], 2) for k in range(n)]

    def swap(values, bit):
        return lax.ppermute(values, "cluster", [(i, i ^ bit) for i in range(n)])

    target = targets(me, positives, counts, order, centroids.shape[0])
    queries = encode(hidden_states, token_ids, up_weight, down_weight)
    for k in reversed(range(bits)):
        queries = jnp.concatenate([queries, swap(queries, 1 << k)], axis=0)
    queries = queries.reshape(-1, queries.shape[-1])
    keep, send, dlogit = score(centroids, queries, target)
    pieces = 4
    grown = []
    for k in range(bits):
        got = swap(send, 1 << k)
        if k < pieces:
            grown = [outer(dlogit, queries, k, pieces, grown)]
        total = keep + got
        half = total.shape[0] // 2
        keep, send = total[:half], total[half:]
    return (total, grown[0])


def solution(mesh):
    placed = (
        P(("groups", "cluster"), None, None),
        P(("groups", "cluster"), None),
        P(),
        P(),
        P("cluster", None),
        P("groups", None),
        P("groups"),
    )
    return jax.shard_map(
        functools.partial(shards, mesh.shape["cluster"]),
        mesh=mesh,
        in_specs=placed,
        out_specs=(P(("groups", "cluster"), None), P(("groups", "cluster"), None)),
        check_vma=False,
    )
```

```python
import functools

import jax
import jax.numpy as jnp
from jax import lax
from jax.experimental import pallas as pl
from jax.experimental.pallas import tpu as pltpu
from jax.sharding import PartitionSpec as P

MB = 32
EPS = 1e-05
F32 = jnp.float32
BF16 = jnp.bfloat16
HBM = pltpu.MemorySpace.HBM
NN = (((1,), (0,)), ((), ()))
NT = (((1,), (1,)), ((), ()))
TN = (((0,), (0,)), ((), ()))


def dot(a, b, dims):
    return lax.dot_general(a, b, dims, preferred_element_type=F32)


def held(count):
    return (pl.BlockSpec(memory_space=pltpu.VMEM),) * count


def far(values):
    return pltpu.with_memory_space_constraint(values, HBM)


def normed(values):
    centered = values - jnp.mean(values, axis=-1, keepdims=True)
    spread = jnp.mean(centered * centered, axis=-1, keepdims=True)
    return centered, lax.rsqrt(spread + EPS)


def mark_targets(rel, target_ref):
    asked, slots = rel.shape
    tiles = target_ref.shape[1] // 128
    entries, rows = 8 * slots, 8 * tiles
    sub = lax.broadcasted_iota(jnp.int32, (8, 1), 0)
    low_at = lax.broadcasted_iota(jnp.int32, (entries, 128), 1)
    row_at = lax.broadcasted_iota(jnp.int32, (entries, rows), 1)
    for q in range(0, asked, 8):
        own = [rel[q : q + 8, s : s + 1] for s in range(slots)]
        low = jnp.concatenate([lax.bitwise_and(r, 127) for r in own], axis=0)
        row = jnp.concatenate([lax.shift_right_arithmetic(r, 7) * 8 + sub for r in own], axis=0)
        lows = jnp.where(low_at == low, 1.0, 0.0).astype(BF16)
        rows_hit = jnp.where(row_at == row, 1.0, 0.0).astype(BF16)
        hits = dot(rows_hit, lows, TN)
        for t in range(tiles):
            target_ref[q : q + 8, t * 128 : (t + 1) * 128] = jnp.where(
                hits[t * 8 : (t + 1) * 8, :] > 0.5, 1.0 / MB, 0.0
            )


def encode_kernel(
    order, c_dev, up_step, x_hbm, ids_hbm, up_hbm, down_hbm, pos_hbm, cnt_hbm, q_ref, target_ref,
    x_ref, ids_ref, up_ref, down_ref, pos_ref, cnt_ref, own_ref, act_ref, sems,
):
    count, length, width = x_ref.shape
    hidden = up_ref.shape[1]
    slots, asked = pos_ref.shape
    me = lax.axis_index("cluster")
    small = [
        pltpu.make_async_copy(src, dst, sems.at[0, k])
        for k, (src, dst) in enumerate([(pos_hbm, pos_ref), (cnt_hbm, cnt_ref), (ids_hbm, ids_ref)])
    ]
    x_copy = pltpu.make_async_copy(x_hbm, x_ref, sems.at[0, 3])
    down_copy = pltpu.make_async_copy(down_hbm, down_ref, sems.at[0, 4])
    ups = []
    for k in range(hidden // up_step):
        cut = (slice(None), pl.ds(k * up_step, up_step))
        ups.append(pltpu.make_async_copy(up_hbm.at[cut], up_ref.at[cut], sems.at[1, k]))
    for copy in small + [x_copy] + ups + [down_copy]:
        copy.start()
    for copy in small:
        copy.wait()
    slot = lax.broadcasted_iota(jnp.int32, (slots, asked), 0)
    rel = jnp.where(slot < cnt_ref[...], pos_ref[...] - me * c_dev, -1).T
    per = own_ref.shape[1]
    for k in range(asked // per):
        own_ref[k] = rel[k * per : (k + 1) * per, :]
    rel = jnp.concatenate([own_ref[lax.bitwise_xor(me, k)] for k in order], axis=0)
    mark_targets(rel, target_ref)
    x_copy.wait()
    x = x_ref[...].reshape(count * length, width)
    for k, copy in enumerate(ups):
        copy.wait()
        cut = slice(k * up_step, (k + 1) * up_step)
        act_ref[:, cut] = jax.nn.gelu(dot(x, up_ref[:, cut], NN)).astype(BF16)
    kept = jnp.sum((ids_ref[...] != 0).astype(F32), axis=1, keepdims=True)
    place = lax.broadcasted_iota(jnp.int32, (length, 1), 0).astype(F32)
    down_copy.wait()
    rows = []
    for k in range(count):
        ffn = dot(act_ref[k * length : (k + 1) * length, :], down_ref[...], NN)
        centered, scale = normed(x_ref[k].astype(F32) + ffn)
        own = kept[k : k + 1, :]
        scale = jnp.where(place < own, scale, 0.0)
        rows.append(jnp.sum(centered * scale, axis=0, keepdims=True) / own)
    centered, scale = normed(jnp.concatenate(rows, axis=0))
    q_ref[...] = (centered * scale).astype(BF16)


def encode(states, ids, up_weight, down_weight, positives, counts, order, c_dev):
    count, length, width = states.shape
    hidden = up_weight.shape[1]
    asked, slots = positives.shape
    up_step = min(512, hidden)
    tokens = count * length
    return pl.pallas_call(
        functools.partial(encode_kernel, order, c_dev, up_step),
        out_shape=(pltpu.VMEM((count, width), BF16), pltpu.VMEM((asked, c_dev), F32)),
        in_specs=[pl.BlockSpec(memory_space=HBM)] * 6,
        out_specs=held(2),
        scratch_shapes=[
            pltpu.VMEM(states.shape, BF16),
            pltpu.VMEM(ids.shape, jnp.int32),
            pltpu.VMEM(up_weight.shape, BF16),
            pltpu.VMEM(down_weight.shape, BF16),
            pltpu.VMEM((slots, asked), jnp.int32),
            pltpu.VMEM((1, asked), jnp.int32),
            pltpu.VMEM((len(order), asked // len(order), slots), jnp.int32),
            pltpu.VMEM((tokens, hidden), BF16),
            pltpu.SemaphoreType.DMA((2, max(5, hidden // up_step))),
        ],
        compiler_params=pltpu.CompilerParams(vmem_limit_bytes=32 << 20),
        cost_estimate=pl.CostEstimate(
            flops=4 * tokens * hidden * width,
            transcendentals=tokens * hidden,
            bytes_accessed=4 * hidden * width + 2 * tokens * width,
        ),
        name="encode",
    )(*map(far, (states, ids, up_weight, down_weight, positives.T, counts.reshape(1, asked))))


def fetch_kernel(first, src_hbm, _, out_ref, mark_ref, sems):
    rows = out_ref.shape[0]
    copy = pltpu.make_async_copy(src_hbm.at[pl.ds(first, rows)], out_ref, sems.at[0])
    copy.start()
    mark_ref[...] = jnp.zeros_like(mark_ref)
    copy.wait()


def fetch(values, first, rows, behind):
    width = values.shape[1]
    return pl.pallas_call(
        functools.partial(fetch_kernel, first),
        out_shape=(pltpu.VMEM((rows, width), values.dtype), pltpu.VMEM((8, 128), F32)),
        in_specs=[pl.BlockSpec(memory_space=HBM), *held(1)],
        out_specs=held(2),
        scratch_shapes=[pltpu.SemaphoreType.DMA((1,))],
        compiler_params=pltpu.CompilerParams(vmem_limit_bytes=4 << 20),
        cost_estimate=pl.CostEstimate(flops=0, transcendentals=0, bytes_accessed=2 * rows * width),
        name="fetch",
    )(far(values), behind)


def join_kernel(a_ref, b_ref, *rest):
    out_ref = rest[-1]
    rows = a_ref.shape[0]
    out_ref[:rows, :] = a_ref[...]
    out_ref[rows:, :] = b_ref[...]


def join(a, b, *behind):
    rows, width = a.shape
    return pl.pallas_call(
        join_kernel,
        out_shape=pltpu.VMEM((2 * rows, width), a.dtype),
        in_specs=held(2 + len(behind)),
        out_specs=pl.BlockSpec(memory_space=pltpu.VMEM),
        compiler_params=pltpu.CompilerParams(vmem_limit_bytes=4 << 20),
        cost_estimate=pl.CostEstimate(flops=0, transcendentals=0, bytes_accessed=1024),
        name="join",
    )(a, b, *behind)


def score_kernel(parts, qa_ref, qb_ref, target_ref, *refs):
    c_refs, (q_ref, keep_ref, send_ref, dlogit_ref) = refs[:parts], refs[parts:]
    half = qa_ref.shape[0]
    q_ref[:half, :] = qa_ref[...]
    q_ref[half:, :] = qb_ref[...]
    queries = q_ref[...]
    first = 0
    for c_ref in c_refs:
        step = min(512, c_ref.shape[0])
        for k in range(c_ref.shape[0] // step):
            logits = dot(c_ref[k * step : (k + 1) * step, :], queries, NT).T
            cut = slice(first, first + step)
            dlogit_ref[:, cut] = (jax.nn.sigmoid(logits) * (1.0 / MB) - target_ref[:, cut]).astype(BF16)
            first += step
    first, grad = 0, 0.0
    for c_ref in c_refs:
        rows = c_ref.shape[0]
        grad += dot(dlogit_ref[:, first : first + rows], c_ref[...], NN)
        first += rows
    keep_ref[...] = grad[:half]
    send_ref[...] = grad[half:]


def score(centroids, qa, qb, target):
    half, width = qa.shape
    count, c_dev = target.shape
    return pl.pallas_call(
        functools.partial(score_kernel, len(centroids)),
        out_shape=(
            pltpu.VMEM((count, width), BF16),
            pltpu.VMEM((half, width), F32),
            pltpu.VMEM((half, width), F32),
            pltpu.VMEM((count, c_dev), BF16),
        ),
        in_specs=held(3 + len(centroids)),
        out_specs=held(4),
        compiler_params=pltpu.CompilerParams(vmem_limit_bytes=32 << 20),
        cost_estimate=pl.CostEstimate(
            flops=4 * count * c_dev * width, transcendentals=count * c_dev, bytes_accessed=2 * c_dev * width
        ),
        name="score",
    )(qa, qb, target, *centroids)


def outer_kernel(first, rows, sub, dlogit_ref, q_ref, *rest):
    out_hbm, held_ref, sems = rest[-3:]
    queries = q_ref[...]
    copies = []
    for k in range(rows // sub):
        cut = slice(k * sub, (k + 1) * sub)
        held_ref[cut, :] = dot(dlogit_ref[:, first + k * sub : first + (k + 1) * sub], queries, TN)
        copies.append(
            pltpu.make_async_copy(held_ref.at[cut], out_hbm.at[pl.ds(first + k * sub, sub)], sems.at[k])
        )
        copies[-1].start()
    for copy in copies:
        copy.wait()


def outer(dlogit, queries, first, rows, grown):
    count, c_dev = dlogit.shape
    width = queries.shape[1]
    sub = min(128, rows)
    return pl.pallas_call(
        functools.partial(outer_kernel, first, rows, sub),
        out_shape=jax.ShapeDtypeStruct((c_dev, width), F32),
        in_specs=[*held(2)] + [pl.BlockSpec(memory_space=HBM)] * len(grown),
        out_specs=pl.BlockSpec(memory_space=HBM),
        scratch_shapes=[pltpu.VMEM((rows, width), F32), pltpu.SemaphoreType.DMA((rows // sub,))],
        input_output_aliases={2: 0} if grown else {},
        compiler_params=pltpu.CompilerParams(vmem_limit_bytes=16 << 20),
        cost_estimate=pl.CostEstimate(
            flops=2 * count * rows * width, transcendentals=0, bytes_accessed=4 * rows * width
        ),
        name="outer",
    )(dlogit, queries, *grown)


def shards(n, hidden_states, token_ids, up_weight, down_weight, centroids, positives, counts):
    bits = n.bit_length() - 1
    order = [int(format(k, f"0{bits}b")[::-1], 2) for k in range(n)]
    c_dev = centroids.shape[0]

    def swap(values, bit):
        return lax.ppermute(values, "cluster", [(i, i ^ bit) for i in range(n)])

    queries, target = encode(
        hidden_states, token_ids, up_weight, down_weight, positives, counts, order, c_dev
    )
    part = c_dev // 2
    fetched = []
    for k in range(bits):
        got = swap(queries, 1 << (bits - 1 - k))
        marks = []
        if k in (1, 2):
            centroid_part, mark = fetch(centroids, (k - 1) * part, part, queries)
            fetched.append(centroid_part)
            marks.append(mark)
        if k < bits - 1:
            queries = join(queries, got, *marks)
    queries, keep, send, dlogit = score(fetched, queries, got, target)
    ends = [round(c_dev // 128 * share) * 128 for share in (0.125, 0.5, 0.78125, 1.0)]
    first, grown = 0, []
    for k in range(bits):
        got = swap(send, 1 << k)
        if k < len(ends) and ends[k] > first:
            grown = [outer(dlogit, queries, first, ends[k] - first, grown)]
            first = ends[k]
            got, grown[0] = lax.optimization_barrier((got, grown[0]))
        total = keep + got
        half = total.shape[0] // 2
        keep, send = total[:half], total[half:]
    return (total, grown[0])


def solution(mesh):
    placed = (
        P(("groups", "cluster"), None, None),
        P(("groups", "cluster"), None),
        P(),
        P(),
        P("cluster", None),
        P("groups", None),
        P("groups"),
    )
    return jax.shard_map(
        functools.partial(shards, mesh.shape["cluster"]),
        mesh=mesh,
        in_specs=placed,
        out_specs=(P(("groups", "cluster"), None), P(("groups", "cluster"), None)),
        check_vma=False,
    )
```

```python
import functools

import jax
import jax.numpy as jnp
from jax import lax
from jax.experimental import pallas as pl
from jax.experimental.pallas import tpu as pltpu
from jax.sharding import PartitionSpec as P

MB = 32
EPS = 1e-05
F32 = jnp.float32
BF16 = jnp.bfloat16
SHARES = (0.0, 0.46875, 0.75, 1.0)
HBM = pltpu.MemorySpace.HBM
NN = (((1,), (0,)), ((), ()))
NT = (((1,), (1,)), ((), ()))
TN = (((0,), (0,)), ((), ()))


def dot(a, b, dims):
    return lax.dot_general(a, b, dims, preferred_element_type=F32)


def held(count):
    return (pl.BlockSpec(memory_space=pltpu.VMEM),) * count


def far(values):
    return pltpu.with_memory_space_constraint(values, HBM)


def normed(values):
    centered = values - jnp.mean(values, axis=-1, keepdims=True)
    spread = jnp.mean(centered * centered, axis=-1, keepdims=True)
    return centered, lax.rsqrt(spread + EPS)


def encode_kernel(
    order, c_dev, up_step, x_hbm, ids_hbm, up_hbm, down_hbm, pos_hbm, cnt_hbm, q_ref, rel_ref,
    x_ref, ids_ref, up_ref, down_ref, pos_ref, cnt_ref, own_ref, act_ref, sems,
):
    count, length, width = x_ref.shape
    hidden = up_ref.shape[1]
    slots, asked = pos_ref.shape
    me = lax.axis_index("cluster")
    small = [
        pltpu.make_async_copy(src, dst, sems.at[0, k])
        for k, (src, dst) in enumerate([(pos_hbm, pos_ref), (cnt_hbm, cnt_ref), (ids_hbm, ids_ref)])
    ]
    x_copy = pltpu.make_async_copy(x_hbm, x_ref, sems.at[0, 3])
    down_copy = pltpu.make_async_copy(down_hbm, down_ref, sems.at[0, 4])
    ups = []
    for k in range(hidden // up_step):
        cut = (slice(None), pl.ds(k * up_step, up_step))
        ups.append(pltpu.make_async_copy(up_hbm.at[cut], up_ref.at[cut], sems.at[1, k]))
    for copy in small + [x_copy] + ups + [down_copy]:
        copy.start()
    for copy in small:
        copy.wait()
    slot = lax.broadcasted_iota(jnp.int32, (slots, asked), 0)
    rel = jnp.where(slot < cnt_ref[...], pos_ref[...] - me * c_dev, -1).T
    per = own_ref.shape[1]
    for k in range(asked // per):
        own_ref[k] = rel[k * per : (k + 1) * per, :]
    rel_ref[...] = jnp.concatenate([own_ref[lax.bitwise_xor(me, k)] for k in order], axis=0)
    x_copy.wait()
    x = x_ref[...].reshape(count * length, width)
    for k, copy in enumerate(ups):
        copy.wait()
        cut = slice(k * up_step, (k + 1) * up_step)
        act_ref[:, cut] = jax.nn.gelu(dot(x, up_ref[:, cut], NN)).astype(BF16)
    kept = jnp.sum((ids_ref[...] != 0).astype(F32), axis=1, keepdims=True)
    place = lax.broadcasted_iota(jnp.int32, (length, 1), 0).astype(F32)
    down_copy.wait()
    rows = []
    for k in range(count):
        ffn = dot(act_ref[k * length : (k + 1) * length, :], down_ref[...], NN)
        centered, scale = normed(x_ref[k].astype(F32) + ffn)
        own = kept[k : k + 1, :]
        scale = jnp.where(place < own, scale, 0.0)
        rows.append(jnp.sum(centered * scale, axis=0, keepdims=True) / own)
    centered, scale = normed(jnp.concatenate(rows, axis=0))
    q_ref[...] = (centered * scale).astype(BF16)


def encode(states, ids, up_weight, down_weight, positives, counts, order, c_dev):
    count, length, width = states.shape
    hidden = up_weight.shape[1]
    asked, slots = positives.shape
    up_step = min(512, hidden)
    tokens = count * length
    return pl.pallas_call(
        functools.partial(encode_kernel, order, c_dev, up_step),
        out_shape=(pltpu.VMEM((count, width), BF16), pltpu.VMEM((asked, slots), jnp.int32)),
        in_specs=[pl.BlockSpec(memory_space=HBM)] * 6,
        out_specs=held(2),
        scratch_shapes=[
            pltpu.VMEM(states.shape, BF16),
            pltpu.VMEM(ids.shape, jnp.int32),
            pltpu.VMEM(up_weight.shape, BF16),
            pltpu.VMEM(down_weight.shape, BF16),
            pltpu.VMEM((slots, asked), jnp.int32),
            pltpu.VMEM((1, asked), jnp.int32),
            pltpu.VMEM((len(order), asked // len(order), slots), jnp.int32),
            pltpu.VMEM((tokens, hidden), BF16),
            pltpu.SemaphoreType.DMA((2, max(5, hidden // up_step))),
        ],
        compiler_params=pltpu.CompilerParams(vmem_limit_bytes=32 << 20),
        cost_estimate=pl.CostEstimate(
            flops=4 * tokens * hidden * width,
            transcendentals=tokens * hidden,
            bytes_accessed=4 * hidden * width + 2 * tokens * width,
        ),
        name="encode",
    )(*map(far, (states, ids, up_weight, down_weight, positives.T, counts.reshape(1, asked))))


def target_kernel(rel_ref, _, target_ref, mark_ref):
    rel = rel_ref[...]
    asked, slots = rel.shape
    mark_ref[...] = jnp.zeros_like(mark_ref)
    tiles = target_ref.shape[1] // 128
    entries, rows = 8 * slots, 8 * tiles
    sub = lax.broadcasted_iota(jnp.int32, (8, 1), 0)
    low_at = lax.broadcasted_iota(jnp.int32, (entries, 128), 1)
    row_at = lax.broadcasted_iota(jnp.int32, (entries, rows), 1)
    for q in range(0, asked, 8):
        own = [rel[q : q + 8, s : s + 1] for s in range(slots)]
        low = jnp.concatenate([lax.bitwise_and(r, 127) for r in own], axis=0)
        row = jnp.concatenate([lax.shift_right_arithmetic(r, 7) * 8 + sub for r in own], axis=0)
        lows = jnp.where(low_at == low, 1.0, 0.0).astype(BF16)
        rows_hit = jnp.where(row_at == row, 1.0, 0.0).astype(BF16)
        hits = dot(rows_hit, lows, TN)
        for t in range(tiles):
            target_ref[q : q + 8, t * 128 : (t + 1) * 128] = jnp.where(
                hits[t * 8 : (t + 1) * 8, :] > 0.5, 1.0 / MB, 0.0
            )


def targets(rel, c_dev, behind):
    asked, slots = rel.shape
    return pl.pallas_call(
        target_kernel,
        out_shape=(pltpu.VMEM((asked, c_dev), F32), pltpu.VMEM((8, 128), F32)),
        in_specs=held(2),
        out_specs=held(2),
        compiler_params=pltpu.CompilerParams(vmem_limit_bytes=8 << 20),
        cost_estimate=pl.CostEstimate(
            flops=16 * asked * slots * c_dev, transcendentals=0, bytes_accessed=4 * asked * c_dev
        ),
        name="targets",
    )(rel, behind)


def fetch_kernel(first, src_hbm, _, out_ref, mark_ref, sems):
    rows = out_ref.shape[0]
    copy = pltpu.make_async_copy(src_hbm.at[pl.ds(first, rows)], out_ref, sems.at[0])
    copy.start()
    mark_ref[...] = jnp.zeros_like(mark_ref)
    copy.wait()


def fetch(values, first, rows, behind):
    width = values.shape[1]
    return pl.pallas_call(
        functools.partial(fetch_kernel, first),
        out_shape=(pltpu.VMEM((rows, width), values.dtype), pltpu.VMEM((8, 128), F32)),
        in_specs=[pl.BlockSpec(memory_space=HBM), *held(1)],
        out_specs=held(2),
        scratch_shapes=[pltpu.SemaphoreType.DMA((1,))],
        compiler_params=pltpu.CompilerParams(vmem_limit_bytes=4 << 20),
        cost_estimate=pl.CostEstimate(flops=0, transcendentals=0, bytes_accessed=2 * rows * width),
        name="fetch",
    )(far(values), behind)


def join_kernel(a_ref, b_ref, *rest):
    out_ref = rest[-1]
    rows = a_ref.shape[0]
    out_ref[:rows, :] = a_ref[...]
    out_ref[rows:, :] = b_ref[...]


def join(a, b, *behind):
    rows, width = a.shape
    return pl.pallas_call(
        join_kernel,
        out_shape=pltpu.VMEM((2 * rows, width), a.dtype),
        in_specs=held(2 + len(behind)),
        out_specs=pl.BlockSpec(memory_space=pltpu.VMEM),
        compiler_params=pltpu.CompilerParams(vmem_limit_bytes=4 << 20),
        cost_estimate=pl.CostEstimate(flops=0, transcendentals=0, bytes_accessed=1024),
        name="join",
    )(a, b, *behind)


def score_kernel(parts, qa_ref, qb_ref, target_ref, *refs):
    c_refs, (q_ref, keep_ref, send_ref, dlogit_ref) = refs[:parts], refs[parts:]
    half = qa_ref.shape[0]
    q_ref[:half, :] = qa_ref[...]
    q_ref[half:, :] = qb_ref[...]
    queries = q_ref[...]
    first = 0
    for c_ref in c_refs:
        step = min(512, c_ref.shape[0])
        for k in range(c_ref.shape[0] // step):
            logits = dot(c_ref[k * step : (k + 1) * step, :], queries, NT).T
            cut = slice(first, first + step)
            dlogit_ref[:, cut] = (jax.nn.sigmoid(logits) * (1.0 / MB) - target_ref[:, cut]).astype(BF16)
            first += step
    first, grad = 0, 0.0
    for c_ref in c_refs:
        rows = c_ref.shape[0]
        grad += dot(dlogit_ref[:, first : first + rows], c_ref[...], NN)
        first += rows
    keep_ref[...] = grad[:half]
    send_ref[...] = grad[half:]


def score(centroids, qa, qb, target):
    half, width = qa.shape
    count, c_dev = target.shape
    return pl.pallas_call(
        functools.partial(score_kernel, len(centroids)),
        out_shape=(
            pltpu.VMEM((count, width), BF16),
            pltpu.VMEM((half, width), F32),
            pltpu.VMEM((half, width), F32),
            pltpu.VMEM((count, c_dev), BF16),
        ),
        in_specs=held(3 + len(centroids)),
        out_specs=held(4),
        compiler_params=pltpu.CompilerParams(vmem_limit_bytes=32 << 20),
        cost_estimate=pl.CostEstimate(
            flops=4 * count * c_dev * width, transcendentals=count * c_dev, bytes_accessed=2 * c_dev * width
        ),
        name="score",
    )(qa, qb, target, *centroids)


def outer_kernel(first, rows, sub, dlogit_ref, q_ref, *rest):
    out_hbm, held_ref, sems = rest[-3:]
    queries = q_ref[...]
    copies = []
    for k in range(rows // sub):
        cut = slice(k * sub, (k + 1) * sub)
        held_ref[cut, :] = dot(dlogit_ref[:, first + k * sub : first + (k + 1) * sub], queries, TN)
        copies.append(
            pltpu.make_async_copy(held_ref.at[cut], out_hbm.at[pl.ds(first + k * sub, sub)], sems.at[k])
        )
        copies[-1].start()
    for copy in copies:
        copy.wait()


def outer(dlogit, queries, first, rows, grown):
    count, c_dev = dlogit.shape
    width = queries.shape[1]
    sub = min(128, rows)
    return pl.pallas_call(
        functools.partial(outer_kernel, first, rows, sub),
        out_shape=jax.ShapeDtypeStruct((c_dev, width), F32),
        in_specs=[*held(2)] + [pl.BlockSpec(memory_space=HBM)] * len(grown),
        out_specs=pl.BlockSpec(memory_space=HBM),
        scratch_shapes=[pltpu.VMEM((rows, width), F32), pltpu.SemaphoreType.DMA((rows // sub,))],
        input_output_aliases={2: 0} if grown else {},
        compiler_params=pltpu.CompilerParams(vmem_limit_bytes=16 << 20),
        cost_estimate=pl.CostEstimate(
            flops=2 * count * rows * width, transcendentals=0, bytes_accessed=4 * rows * width
        ),
        name="outer",
    )(dlogit, queries, *grown)


def shards(n, hidden_states, token_ids, up_weight, down_weight, centroids, positives, counts):
    bits = n.bit_length() - 1
    pairs = [1] + [1 << k | 1 for k in range(1, bits)]
    order = [0]
    for pair in reversed(pairs):
        order += [k ^ pair for k in order]
    c_dev = centroids.shape[0]

    def swap(values, pair):
        return lax.ppermute(values, "cluster", [(i, i ^ pair) for i in range(n)])

    queries, rel = encode(
        hidden_states, token_ids, up_weight, down_weight, positives, counts, order, c_dev
    )
    part = c_dev // 2
    fetched = []
    for k, pair in enumerate(reversed(pairs)):
        got = swap(queries, pair)
        marks = []
        if k == min(2, bits - 2):
            target, mark = targets(rel, c_dev, queries)
            marks.append(mark)
        if k < 2:
            centroid_part, mark = fetch(centroids, k * part, part, queries)
            fetched.append(centroid_part)
            marks.append(mark)
        if k < bits - 1:
            queries = join(queries, got, *marks)
    queries, keep, send, dlogit = score(fetched, queries, got, target)
    ends = [round(c_dev // 128 * share) * 128 for share in SHARES]
    first, grown = 0, []
    for k, pair in enumerate(pairs):
        got = swap(send, pair)
        if k < len(ends) and ends[k] > first:
            grown = [outer(dlogit, queries, first, ends[k] - first, grown)]
            first = ends[k]
            got, grown[0] = lax.optimization_barrier((got, grown[0]))
        total = keep + got
        half = total.shape[0] // 2
        keep, send = total[:half], total[half:]
    return (total, grown[0])


def solution(mesh):
    placed = (
        P(("groups", "cluster"), None, None),
        P(("groups", "cluster"), None),
        P(),
        P(),
        P("cluster", None),
        P("groups", None),
        P("groups"),
    )
    return jax.shard_map(
        functools.partial(shards, mesh.shape["cluster"]),
        mesh=mesh,
        in_specs=placed,
        out_specs=(P(("groups", "cluster"), None), P(("groups", "cluster"), None)),
        check_vma=False,
    )
```

```python
import functools

import jax
import jax.numpy as jnp
from jax import lax
from jax.experimental import pallas as pl
from jax.experimental.pallas import tpu as pltpu
from jax.sharding import PartitionSpec as P

MB = 32
EPS = 1e-05
F32 = jnp.float32
BF16 = jnp.bfloat16
FETCH = (0.0, 0.3125, 0.6875, 1.0)
SHARES = (0.0, 0.46875, 0.75, 1.0)
HBM = pltpu.MemorySpace.HBM
NN = (((1,), (0,)), ((), ()))
NT = (((1,), (1,)), ((), ()))
TN = (((0,), (0,)), ((), ()))


def dot(a, b, dims):
    return lax.dot_general(a, b, dims, preferred_element_type=F32)


def held(count):
    return (pl.BlockSpec(memory_space=pltpu.VMEM),) * count


def far(values):
    return pltpu.with_memory_space_constraint(values, HBM)


def normed(values):
    centered = values - jnp.mean(values, axis=-1, keepdims=True)
    spread = jnp.mean(centered * centered, axis=-1, keepdims=True)
    return centered, lax.rsqrt(spread + EPS)


def mark_targets(rel, first, asked, target_ref):
    slots = rel.shape[1]
    tiles = target_ref.shape[1] // 128
    entries, rows = 8 * slots, 8 * tiles
    sub = lax.broadcasted_iota(jnp.int32, (8, 1), 0)
    low_at = lax.broadcasted_iota(jnp.int32, (entries, 128), 1)
    row_at = lax.broadcasted_iota(jnp.int32, (entries, rows), 1)
    for q in range(first, first + asked, 8):
        own = [rel[q : q + 8, s : s + 1] for s in range(slots)]
        low = jnp.concatenate([lax.bitwise_and(r, 127) for r in own], axis=0)
        row = jnp.concatenate([lax.shift_right_arithmetic(r, 7) * 8 + sub for r in own], axis=0)
        lows = jnp.where(low_at == low, 1.0, 0.0).astype(BF16)
        rows_hit = jnp.where(row_at == row, 1.0, 0.0).astype(BF16)
        hits = dot(rows_hit, lows, TN)
        for t in range(tiles):
            target_ref[q : q + 8, t * 128 : (t + 1) * 128] = jnp.where(
                hits[t * 8 : (t + 1) * 8, :] > 0.5, 1.0 / MB, 0.0
            )


def encode_kernel(
    order, c_dev, up_step, x_hbm, ids_hbm, up_hbm, down_hbm, pos_hbm, cnt_hbm, q_ref, target_ref,
    x_ref, ids_ref, up_ref, down_ref, pos_ref, cnt_ref, own_ref, act_ref, sems,
):
    count, length, width = x_ref.shape
    hidden = up_ref.shape[1]
    slots, asked = pos_ref.shape
    me = lax.axis_index("cluster")
    small = [
        pltpu.make_async_copy(src, dst, sems.at[0, k])
        for k, (src, dst) in enumerate([(pos_hbm, pos_ref), (cnt_hbm, cnt_ref), (ids_hbm, ids_ref)])
    ]
    x_copy = pltpu.make_async_copy(x_hbm, x_ref, sems.at[0, 3])
    down_copy = pltpu.make_async_copy(down_hbm, down_ref, sems.at[0, 4])
    ups = []
    for k in range(hidden // up_step):
        cut = (slice(None), pl.ds(k * up_step, up_step))
        ups.append(pltpu.make_async_copy(up_hbm.at[cut], up_ref.at[cut], sems.at[1, k]))
    for copy in small + [x_copy] + ups + [down_copy]:
        copy.start()
    for copy in small:
        copy.wait()
    slot = lax.broadcasted_iota(jnp.int32, (slots, asked), 0)
    rel = jnp.where(slot < cnt_ref[...], pos_ref[...] - me * c_dev, -1).T
    per = own_ref.shape[1]
    for k in range(asked // per):
        own_ref[k] = rel[k * per : (k + 1) * per, :]
    rel = jnp.concatenate([own_ref[lax.bitwise_xor(me, k)] for k in order], axis=0)
    x_copy.wait()
    x = x_ref[...].reshape(count * length, width)
    for k, copy in enumerate(ups):
        copy.wait()
        cut = slice(k * up_step, (k + 1) * up_step)
        act_ref[:, cut] = jax.nn.gelu(dot(x, up_ref[:, cut], NN)).astype(BF16)
        share = asked // len(ups)
        mark_targets(rel, k * share, share, target_ref)
    kept = jnp.sum((ids_ref[...] != 0).astype(F32), axis=1, keepdims=True)
    place = lax.broadcasted_iota(jnp.int32, (length, 1), 0).astype(F32)
    down_copy.wait()
    rows = []
    for k in range(count):
        ffn = dot(act_ref[k * length : (k + 1) * length, :], down_ref[...], NN)
        centered, scale = normed(x_ref[k].astype(F32) + ffn)
        own = kept[k : k + 1, :]
        scale = jnp.where(place < own, scale, 0.0)
        rows.append(jnp.sum(centered * scale, axis=0, keepdims=True) / own)
    centered, scale = normed(jnp.concatenate(rows, axis=0))
    q_ref[...] = (centered * scale).astype(BF16)


def encode(states, ids, up_weight, down_weight, positives, counts, order, c_dev):
    count, length, width = states.shape
    hidden = up_weight.shape[1]
    asked, slots = positives.shape
    up_step = min(512, hidden)
    tokens = count * length
    return pl.pallas_call(
        functools.partial(encode_kernel, order, c_dev, up_step),
        out_shape=(pltpu.VMEM((count, width), BF16), pltpu.VMEM((asked, c_dev), F32)),
        in_specs=[pl.BlockSpec(memory_space=HBM)] * 6,
        out_specs=held(2),
        scratch_shapes=[
            pltpu.VMEM(states.shape, BF16),
            pltpu.VMEM(ids.shape, jnp.int32),
            pltpu.VMEM(up_weight.shape, BF16),
            pltpu.VMEM(down_weight.shape, BF16),
            pltpu.VMEM((slots, asked), jnp.int32),
            pltpu.VMEM((1, asked), jnp.int32),
            pltpu.VMEM((len(order), asked // len(order), slots), jnp.int32),
            pltpu.VMEM((tokens, hidden), BF16),
            pltpu.SemaphoreType.DMA((2, max(5, hidden // up_step))),
        ],
        compiler_params=pltpu.CompilerParams(vmem_limit_bytes=32 << 20),
        cost_estimate=pl.CostEstimate(
            flops=4 * tokens * hidden * width,
            transcendentals=tokens * hidden,
            bytes_accessed=4 * hidden * width + 2 * tokens * width,
        ),
        name="encode",
    )(*map(far, (states, ids, up_weight, down_weight, positives.T, counts.reshape(1, asked))))


def fetch_kernel(first, sub, src_hbm, _, out_ref, flip_ref, mark_ref, sems):
    copies = []
    for k in range(out_ref.shape[0] // sub):
        copies.append(
            pltpu.make_async_copy(
                src_hbm.at[pl.ds(first + k * sub, sub)], out_ref.at[pl.ds(k * sub, sub)], sems.at[k]
            )
        )
        copies[-1].start()
    mark_ref[...] = jnp.zeros_like(mark_ref)
    for k, copy in enumerate(copies):
        copy.wait()
        cut = slice(k * sub, (k + 1) * sub)
        flip_ref[:, cut] = out_ref[cut, :].T


def fetch(values, first, rows, behind):
    width = values.shape[1]
    sub = min(256, rows)
    return pl.pallas_call(
        functools.partial(fetch_kernel, first, sub),
        out_shape=(
            pltpu.VMEM((rows, width), values.dtype),
            pltpu.VMEM((width, rows), values.dtype),
            pltpu.VMEM((8, 128), F32),
        ),
        in_specs=[pl.BlockSpec(memory_space=HBM), *held(1)],
        out_specs=held(3),
        scratch_shapes=[pltpu.SemaphoreType.DMA((rows // sub,))],
        compiler_params=pltpu.CompilerParams(vmem_limit_bytes=4 << 20),
        cost_estimate=pl.CostEstimate(flops=0, transcendentals=0, bytes_accessed=2 * rows * width),
        name="fetch",
    )(far(values), behind)


def join_kernel(a_ref, b_ref, *rest):
    out_ref = rest[-1]
    rows = a_ref.shape[0]
    out_ref[:rows, :] = a_ref[...]
    out_ref[rows:, :] = b_ref[...]


def join(a, b, *behind):
    rows, width = a.shape
    return pl.pallas_call(
        join_kernel,
        out_shape=pltpu.VMEM((2 * rows, width), a.dtype),
        in_specs=held(2 + len(behind)),
        out_specs=pl.BlockSpec(memory_space=pltpu.VMEM),
        compiler_params=pltpu.CompilerParams(vmem_limit_bytes=4 << 20),
        cost_estimate=pl.CostEstimate(flops=0, transcendentals=0, bytes_accessed=1024),
        name="join",
    )(a, b, *behind)


def score_kernel(parts, qa_ref, qb_ref, target_ref, *refs):
    c_refs, flip_refs = refs[:parts], refs[parts : 2 * parts]
    q_ref, keep_ref, send_ref, dlogit_ref = refs[2 * parts :]
    half = qa_ref.shape[0]
    q_ref[:half, :] = qa_ref[...]
    q_ref[half:, :] = qb_ref[...]
    queries = q_ref[...]
    first = 0
    for flip_ref in flip_refs:
        columns = flip_ref.shape[1]
        for k in range(0, columns, 512):
            step = min(512, columns - k)
            logits = dot(queries, flip_ref[:, k : k + step], NN)
            cut = slice(first, first + step)
            dlogit_ref[:, cut] = (jax.nn.sigmoid(logits) * (1.0 / MB) - target_ref[:, cut]).astype(BF16)
            first += step
    first, grad = 0, 0.0
    for c_ref in c_refs:
        rows = c_ref.shape[0]
        grad += dot(dlogit_ref[:, first : first + rows], c_ref[...], NN)
        first += rows
    keep_ref[...] = grad[:half]
    send_ref[...] = grad[half:]


def score(centroids, flipped, qa, qb, target):
    half, width = qa.shape
    count, c_dev = target.shape
    return pl.pallas_call(
        functools.partial(score_kernel, len(centroids)),
        out_shape=(
            pltpu.VMEM((count, width), BF16),
            pltpu.VMEM((half, width), F32),
            pltpu.VMEM((half, width), F32),
            pltpu.VMEM((count, c_dev), BF16),
        ),
        in_specs=held(3 + 2 * len(centroids)),
        out_specs=held(4),
        compiler_params=pltpu.CompilerParams(vmem_limit_bytes=32 << 20),
        cost_estimate=pl.CostEstimate(
            flops=4 * count * c_dev * width, transcendentals=count * c_dev, bytes_accessed=2 * c_dev * width
        ),
        name="score",
    )(qa, qb, target, *centroids, *flipped)


def outer_kernel(first, rows, sub, dlogit_ref, q_ref, *rest):
    out_hbm, held_ref, sems = rest[-3:]
    queries = q_ref[...]
    copies = []
    for k in range(rows // sub):
        cut = slice(k * sub, (k + 1) * sub)
        held_ref[cut, :] = dot(dlogit_ref[:, first + k * sub : first + (k + 1) * sub], queries, TN)
        copies.append(
            pltpu.make_async_copy(held_ref.at[cut], out_hbm.at[pl.ds(first + k * sub, sub)], sems.at[k])
        )
        copies[-1].start()
    for copy in copies:
        copy.wait()


def outer(dlogit, queries, first, rows, grown):
    count, c_dev = dlogit.shape
    width = queries.shape[1]
    sub = min(128, rows)
    return pl.pallas_call(
        functools.partial(outer_kernel, first, rows, sub),
        out_shape=jax.ShapeDtypeStruct((c_dev, width), F32),
        in_specs=[*held(2)] + [pl.BlockSpec(memory_space=HBM)] * len(grown),
        out_specs=pl.BlockSpec(memory_space=HBM),
        scratch_shapes=[pltpu.VMEM((rows, width), F32), pltpu.SemaphoreType.DMA((rows // sub,))],
        input_output_aliases={2: 0} if grown else {},
        compiler_params=pltpu.CompilerParams(vmem_limit_bytes=16 << 20),
        cost_estimate=pl.CostEstimate(
            flops=2 * count * rows * width, transcendentals=0, bytes_accessed=4 * rows * width
        ),
        name="outer",
    )(dlogit, queries, *grown)


def shards(n, hidden_states, token_ids, up_weight, down_weight, centroids, positives, counts):
    bits = n.bit_length() - 1
    pairs = [1] + [1 << k | 1 for k in range(1, bits)]
    order = [0]
    for pair in reversed(pairs):
        order += [k ^ pair for k in order]
    c_dev = centroids.shape[0]

    def swap(values, pair):
        return lax.ppermute(values, "cluster", [(i, i ^ pair) for i in range(n)])

    queries, target = encode(
        hidden_states, token_ids, up_weight, down_weight, positives, counts, order, c_dev
    )
    cuts = [round(c_dev // 256 * share) * 256 for share in FETCH]
    fetched, flipped = [], []
    for k, pair in enumerate(reversed(pairs)):
        got = swap(queries, pair)
        marks = []
        if k < len(cuts) - 1 and cuts[k + 1] > cuts[k]:
            part, flip, mark = fetch(centroids, cuts[k], cuts[k + 1] - cuts[k], queries)
            fetched.append(part)
            flipped.append(flip)
            marks.append(mark)
        if k < bits - 1:
            queries = join(queries, got, *marks)
    queries, keep, send, dlogit = score(fetched, flipped, queries, got, target)
    ends = [round(c_dev // 128 * share) * 128 for share in SHARES]
    first, grown = 0, []
    for k, pair in enumerate(pairs):
        got = swap(send, pair)
        if k < len(ends) and ends[k] > first:
            grown = [outer(dlogit, queries, first, ends[k] - first, grown)]
            first = ends[k]
            got, grown[0] = lax.optimization_barrier((got, grown[0]))
        total = keep + got
        half = total.shape[0] // 2
        keep, send = total[:half], total[half:]
    return (total, grown[0])


def solution(mesh):
    placed = (
        P(("groups", "cluster"), None, None),
        P(("groups", "cluster"), None),
        P(),
        P(),
        P("cluster", None),
        P("groups", None),
        P("groups"),
    )
    return jax.shard_map(
        functools.partial(shards, mesh.shape["cluster"]),
        mesh=mesh,
        in_specs=placed,
        out_specs=(P(("groups", "cluster"), None), P(("groups", "cluster"), None)),
        check_vma=False,
    )
```

```python
import functools

import jax
import jax.numpy as jnp
from jax import lax
from jax.experimental import pallas as pl
from jax.experimental.pallas import tpu as pltpu
from jax.sharding import PartitionSpec as P

MB = 32
EPS = 1e-05
F32 = jnp.float32
BF16 = jnp.bfloat16
FETCH = (0.0, 0.3125, 0.6875, 1.0)
FIRST = 0.25
SHARES = (0.0, 0.5625, 0.78125, 1.0)
HBM = pltpu.MemorySpace.HBM
NN = (((1,), (0,)), ((), ()))
NT = (((1,), (1,)), ((), ()))
TN = (((0,), (0,)), ((), ()))


def dot(a, b, dims):
    return lax.dot_general(a, b, dims, preferred_element_type=F32)


def held(count):
    return (pl.BlockSpec(memory_space=pltpu.VMEM),) * count


def far(values):
    return pltpu.with_memory_space_constraint(values, HBM)


def normed(values):
    centered = values - jnp.mean(values, axis=-1, keepdims=True)
    spread = jnp.mean(centered * centered, axis=-1, keepdims=True)
    return centered, lax.rsqrt(spread + EPS)


def mark_targets(rel, first, asked, target_ref):
    slots = rel.shape[1]
    tiles = target_ref.shape[1] // 128
    entries, rows = 8 * slots, 8 * tiles
    sub = lax.broadcasted_iota(jnp.int32, (8, 1), 0)
    low_at = lax.broadcasted_iota(jnp.int32, (entries, 128), 1)
    row_at = lax.broadcasted_iota(jnp.int32, (entries, rows), 1)
    for q in range(first, first + asked, 8):
        own = [rel[q : q + 8, s : s + 1] for s in range(slots)]
        low = jnp.concatenate([lax.bitwise_and(r, 127) for r in own], axis=0)
        row = jnp.concatenate([lax.shift_right_arithmetic(r, 7) * 8 + sub for r in own], axis=0)
        lows = jnp.where(low_at == low, 1.0, 0.0).astype(BF16)
        rows_hit = jnp.where(row_at == row, 1.0, 0.0).astype(BF16)
        hits = dot(rows_hit, lows, TN)
        for t in range(tiles):
            target_ref[q : q + 8, t * 128 : (t + 1) * 128] = jnp.where(
                hits[t * 8 : (t + 1) * 8, :] > 0.5, 1.0 / MB, 0.0
            )


def encode_kernel(
    order, c_dev, up_step, x_hbm, ids_hbm, up_hbm, down_hbm, pos_hbm, cnt_hbm, q_ref, target_ref,
    x_ref, ids_ref, up_ref, down_ref, pos_ref, cnt_ref, own_ref, act_ref, sems,
):
    count, length, width = x_ref.shape
    hidden = up_ref.shape[1]
    slots, asked = pos_ref.shape
    me = lax.axis_index("cluster")
    small = [
        pltpu.make_async_copy(src, dst, sems.at[0, k])
        for k, (src, dst) in enumerate([(pos_hbm, pos_ref), (cnt_hbm, cnt_ref), (ids_hbm, ids_ref)])
    ]
    x_copy = pltpu.make_async_copy(x_hbm, x_ref, sems.at[0, 3])
    down_copy = pltpu.make_async_copy(down_hbm, down_ref, sems.at[0, 4])
    ups = []
    for k in range(hidden // up_step):
        cut = (slice(None), pl.ds(k * up_step, up_step))
        ups.append(pltpu.make_async_copy(up_hbm.at[cut], up_ref.at[cut], sems.at[1, k]))
    for copy in small + [x_copy] + ups + [down_copy]:
        copy.start()
    for copy in small:
        copy.wait()
    slot = lax.broadcasted_iota(jnp.int32, (slots, asked), 0)
    rel = jnp.where(slot < cnt_ref[...], pos_ref[...] - me * c_dev, -1).T
    per = own_ref.shape[1]
    for k in range(asked // per):
        own_ref[k] = rel[k * per : (k + 1) * per, :]
    rel = jnp.concatenate([own_ref[lax.bitwise_xor(me, k)] for k in order], axis=0)
    x_copy.wait()
    x = x_ref[...].reshape(count * length, width)
    for k, copy in enumerate(ups):
        copy.wait()
        cut = slice(k * up_step, (k + 1) * up_step)
        act_ref[:, cut] = jax.nn.gelu(dot(x, up_ref[:, cut], NN)).astype(BF16)
        share = asked // len(ups)
        mark_targets(rel, k * share, share, target_ref)
    kept = jnp.sum((ids_ref[...] != 0).astype(F32), axis=1, keepdims=True)
    place = lax.broadcasted_iota(jnp.int32, (length, 1), 0).astype(F32)
    down_copy.wait()
    rows = []
    for k in range(count):
        ffn = dot(act_ref[k * length : (k + 1) * length, :], down_ref[...], NN)
        centered, scale = normed(x_ref[k].astype(F32) + ffn)
        own = kept[k : k + 1, :]
        scale = jnp.where(place < own, scale, 0.0)
        rows.append(jnp.sum(centered * scale, axis=0, keepdims=True) / own)
    centered, scale = normed(jnp.concatenate(rows, axis=0))
    q_ref[...] = (centered * scale).astype(BF16)


def encode(states, ids, up_weight, down_weight, positives, counts, order, c_dev):
    count, length, width = states.shape
    hidden = up_weight.shape[1]
    asked, slots = positives.shape
    up_step = min(512, hidden)
    tokens = count * length
    return pl.pallas_call(
        functools.partial(encode_kernel, order, c_dev, up_step),
        out_shape=(pltpu.VMEM((count, width), BF16), pltpu.VMEM((asked, c_dev), F32)),
        in_specs=[pl.BlockSpec(memory_space=HBM)] * 6,
        out_specs=held(2),
        scratch_shapes=[
            pltpu.VMEM(states.shape, BF16),
            pltpu.VMEM(ids.shape, jnp.int32),
            pltpu.VMEM(up_weight.shape, BF16),
            pltpu.VMEM(down_weight.shape, BF16),
            pltpu.VMEM((slots, asked), jnp.int32),
            pltpu.VMEM((1, asked), jnp.int32),
            pltpu.VMEM((len(order), asked // len(order), slots), jnp.int32),
            pltpu.VMEM((tokens, hidden), BF16),
            pltpu.SemaphoreType.DMA((2, max(5, hidden // up_step))),
        ],
        compiler_params=pltpu.CompilerParams(vmem_limit_bytes=32 << 20),
        cost_estimate=pl.CostEstimate(
            flops=4 * tokens * hidden * width,
            transcendentals=tokens * hidden,
            bytes_accessed=4 * hidden * width + 2 * tokens * width,
        ),
        name="encode",
    )(*map(far, (states, ids, up_weight, down_weight, positives.T, counts.reshape(1, asked))))


def flip_kernel(first, src_ref, _, flip_ref, mark_ref):
    mark_ref[...] = jnp.zeros_like(mark_ref)
    rows = flip_ref.shape[1]
    sub = min(256, rows)
    for k in range(0, rows, sub):
        flip_ref[:, k : k + sub] = src_ref[first + k : first + k + sub, :].T


def flip(values, first, rows, behind):
    width = values.shape[1]
    return pl.pallas_call(
        functools.partial(flip_kernel, first),
        out_shape=(pltpu.VMEM((width, rows), values.dtype), pltpu.VMEM((8, 128), F32)),
        in_specs=held(2),
        out_specs=held(2),
        compiler_params=pltpu.CompilerParams(vmem_limit_bytes=4 << 20),
        cost_estimate=pl.CostEstimate(flops=0, transcendentals=0, bytes_accessed=2 * rows * width),
        name="flip",
    )(values, behind)


def join_kernel(a_ref, b_ref, *rest):
    out_ref = rest[-1]
    rows = a_ref.shape[0]
    out_ref[:rows, :] = a_ref[...]
    out_ref[rows:, :] = b_ref[...]


def join(a, b, *behind):
    rows, width = a.shape
    return pl.pallas_call(
        join_kernel,
        out_shape=pltpu.VMEM((2 * rows, width), a.dtype),
        in_specs=held(2 + len(behind)),
        out_specs=pl.BlockSpec(memory_space=pltpu.VMEM),
        compiler_params=pltpu.CompilerParams(vmem_limit_bytes=4 << 20),
        cost_estimate=pl.CostEstimate(flops=0, transcendentals=0, bytes_accessed=1024),
        name="join",
    )(a, b, *behind)


def outer_copies(first, rows, dlogit_ref, queries, out_hbm, held_ref, sems):
    copies = []
    for k in range(rows // 128):
        cut = slice(k * 128, (k + 1) * 128)
        held_ref[cut, :] = dot(dlogit_ref[:, first + k * 128 : first + (k + 1) * 128], queries, TN)
        copies.append(
            pltpu.make_async_copy(held_ref.at[cut], out_hbm.at[pl.ds(first + k * 128, 128)], sems.at[k])
        )
        copies[-1].start()
    return copies


def score_kernel(parts, qa_ref, qb_ref, target_ref, c_ref, *refs):
    flip_refs, (q_ref, keep_ref, send_ref, dlogit_ref, out_hbm, held_ref, sems) = refs[:parts], refs[parts:]
    half = qa_ref.shape[0]
    q_ref[:half, :] = qa_ref[...]
    q_ref[half:, :] = qb_ref[...]
    queries = q_ref[...]
    first = 0
    for flip_ref in flip_refs:
        columns = flip_ref.shape[1]
        for k in range(0, columns, 512):
            step = min(512, columns - k)
            logits = dot(queries, flip_ref[:, k : k + step], NN)
            cut = slice(first, first + step)
            dlogit_ref[:, cut] = (jax.nn.sigmoid(logits) * (1.0 / MB) - target_ref[:, cut]).astype(BF16)
            first += step
    copies = outer_copies(0, held_ref.shape[0], dlogit_ref, queries, out_hbm, held_ref, sems)
    grad = dot(dlogit_ref[...], c_ref[...], NN)
    keep_ref[...] = grad[:half]
    send_ref[...] = grad[half:]
    for copy in copies:
        copy.wait()


def score(centroids, flipped, qa, qb, target, rows):
    half, width = qa.shape
    count, c_dev = target.shape
    return pl.pallas_call(
        functools.partial(score_kernel, len(flipped)),
        out_shape=(
            pltpu.VMEM((count, width), BF16),
            pltpu.VMEM((half, width), F32),
            pltpu.VMEM((half, width), F32),
            pltpu.VMEM((count, c_dev), BF16),
            jax.ShapeDtypeStruct((c_dev, width), F32),
        ),
        in_specs=held(4 + len(flipped)),
        out_specs=(*held(4), pl.BlockSpec(memory_space=HBM)),
        scratch_shapes=[pltpu.VMEM((rows, width), F32), pltpu.SemaphoreType.DMA((rows // 128,))],
        compiler_params=pltpu.CompilerParams(vmem_limit_bytes=32 << 20),
        cost_estimate=pl.CostEstimate(
            flops=4 * count * c_dev * width, transcendentals=count * c_dev, bytes_accessed=2 * c_dev * width
        ),
        name="score",
    )(qa, qb, target, centroids, *flipped)


def outer_kernel(first, rows, dlogit_ref, q_ref, _, out_hbm, held_ref, sems):
    for copy in outer_copies(first, rows, dlogit_ref, q_ref[...], out_hbm, held_ref, sems):
        copy.wait()


def outer(dlogit, queries, first, rows, grown):
    count, c_dev = dlogit.shape
    width = queries.shape[1]
    return pl.pallas_call(
        functools.partial(outer_kernel, first, rows),
        out_shape=jax.ShapeDtypeStruct((c_dev, width), F32),
        in_specs=[*held(2), pl.BlockSpec(memory_space=HBM)],
        out_specs=pl.BlockSpec(memory_space=HBM),
        scratch_shapes=[pltpu.VMEM((rows, width), F32), pltpu.SemaphoreType.DMA((rows // 128,))],
        input_output_aliases={2: 0},
        compiler_params=pltpu.CompilerParams(vmem_limit_bytes=16 << 20),
        cost_estimate=pl.CostEstimate(
            flops=2 * count * rows * width, transcendentals=0, bytes_accessed=4 * rows * width
        ),
        name="outer",
    )(dlogit, queries, grown)


def shards(n, hidden_states, token_ids, up_weight, down_weight, centroids, positives, counts):
    bits = n.bit_length() - 1
    pairs = [1] + [1 << k | 1 for k in range(1, bits)]
    order = [0]
    for pair in reversed(pairs):
        order += [k ^ pair for k in order]
    c_dev = centroids.shape[0]

    def swap(values, pair):
        return lax.ppermute(values, "cluster", [(i, i ^ pair) for i in range(n)])

    queries, target = encode(
        hidden_states, token_ids, up_weight, down_weight, positives, counts, order, c_dev
    )
    cuts = [round(c_dev // 256 * share) * 256 for share in FETCH]
    flipped = []
    for k, pair in enumerate(reversed(pairs)):
        got = swap(queries, pair)
        marks = []
        if k < len(cuts) - 1 and cuts[k + 1] > cuts[k]:
            part, mark = flip(centroids, cuts[k], cuts[k + 1] - cuts[k], queries)
            flipped.append(part)
            marks.append(mark)
        if k < bits - 1:
            queries = join(queries, got, *marks)
    ends = [round(c_dev // 128 * share) * 128 for share in SHARES]
    first = max(128, round(c_dev // 128 * FIRST) * 128)
    queries, keep, send, dlogit, grown = score(centroids, flipped, queries, got, target, first)
    for k, pair in enumerate(pairs):
        got = swap(send, pair)
        if k < len(ends) and ends[k] > first:
            grown = outer(dlogit, queries, first, ends[k] - first, grown)
            first = ends[k]
            got, grown = lax.optimization_barrier((got, grown))
        total = keep + got
        half = total.shape[0] // 2
        keep, send = total[:half], total[half:]
    return (total, grown)


def solution(mesh):
    placed = (
        P(("groups", "cluster"), None, None),
        P(("groups", "cluster"), None),
        P(),
        P(),
        P("cluster", None),
        P("groups", None),
        P("groups"),
    )
    return jax.shard_map(
        functools.partial(shards, mesh.shape["cluster"]),
        mesh=mesh,
        in_specs=placed,
        out_specs=(P(("groups", "cluster"), None), P(("groups", "cluster"), None)),
        check_vma=False,
    )
```

```python
import functools

import jax
import jax.numpy as jnp
from jax import lax
from jax.experimental import pallas as pl
from jax.experimental.pallas import tpu as pltpu
from jax.sharding import PartitionSpec as P

MB = 32
EPS = 1e-05
F32 = jnp.float32
BF16 = jnp.bfloat16
FETCH = (0.0, 0.3125, 0.6875, 1.0)
FIRST = 0.25
SHARES = (0.0, 0.59375, 0.84375, 1.0)
HBM = pltpu.MemorySpace.HBM
NN = (((1,), (0,)), ((), ()))
NT = (((1,), (1,)), ((), ()))
TN = (((0,), (0,)), ((), ()))


def dot(a, b, dims):
    return lax.dot_general(a, b, dims, preferred_element_type=F32)


def held(count):
    return (pl.BlockSpec(memory_space=pltpu.VMEM),) * count


def far(values):
    return pltpu.with_memory_space_constraint(values, HBM)


def normed(values):
    centered = values - jnp.mean(values, axis=-1, keepdims=True)
    spread = jnp.mean(centered * centered, axis=-1, keepdims=True)
    return centered, lax.rsqrt(spread + EPS)


def mark_targets(rel, first, asked, target_ref):
    slots = rel.shape[1]
    tiles = target_ref.shape[1] // 128
    entries, rows = 8 * slots, 8 * tiles
    sub = lax.broadcasted_iota(jnp.int32, (8, 1), 0)
    low_at = lax.broadcasted_iota(jnp.int32, (entries, 128), 1)
    row_at = lax.broadcasted_iota(jnp.int32, (entries, rows), 1)
    for q in range(first, first + asked, 8):
        own = [rel[q : q + 8, s : s + 1] for s in range(slots)]
        low = jnp.concatenate([lax.bitwise_and(r, 127) for r in own], axis=0)
        row = jnp.concatenate([lax.shift_right_arithmetic(r, 7) * 8 + sub for r in own], axis=0)
        lows = jnp.where(low_at == low, 1.0, 0.0).astype(BF16)
        rows_hit = jnp.where(row_at == row, 1.0, 0.0).astype(BF16)
        hits = dot(rows_hit, lows, TN)
        for t in range(tiles):
            target_ref[q : q + 8, t * 128 : (t + 1) * 128] = jnp.where(
                hits[t * 8 : (t + 1) * 8, :] > 0.5, 1.0 / MB, 0.0
            )


def encode_kernel(
    order, c_dev, up_step, x_hbm, ids_hbm, up_hbm, down_hbm, pos_hbm, cnt_hbm, q_ref, target_ref,
    x_ref, ids_ref, up_ref, down_ref, pos_ref, cnt_ref, own_ref, act_ref, sems,
):
    count, length, width = x_ref.shape
    hidden = up_ref.shape[1]
    slots, asked = pos_ref.shape
    me = lax.axis_index("cluster")
    small = [
        pltpu.make_async_copy(src, dst, sems.at[0, k])
        for k, (src, dst) in enumerate([(pos_hbm, pos_ref), (cnt_hbm, cnt_ref), (ids_hbm, ids_ref)])
    ]
    x_copy = pltpu.make_async_copy(x_hbm, x_ref, sems.at[0, 3])
    down_copy = pltpu.make_async_copy(down_hbm, down_ref, sems.at[0, 4])
    ups = []
    for k in range(hidden // up_step):
        cut = (slice(None), pl.ds(k * up_step, up_step))
        ups.append(pltpu.make_async_copy(up_hbm.at[cut], up_ref.at[cut], sems.at[1, k]))
    for copy in small + [x_copy] + ups + [down_copy]:
        copy.start()
    for copy in small:
        copy.wait()
    slot = lax.broadcasted_iota(jnp.int32, (slots, asked), 0)
    rel = jnp.where(slot < cnt_ref[...], pos_ref[...] - me * c_dev, -1).T
    per = own_ref.shape[1]
    for k in range(asked // per):
        own_ref[k] = rel[k * per : (k + 1) * per, :]
    rel = jnp.concatenate([own_ref[lax.bitwise_xor(me, k)] for k in order], axis=0)
    x_copy.wait()
    x = x_ref[...].reshape(count * length, width)
    for k, copy in enumerate(ups):
        copy.wait()
        cut = slice(k * up_step, (k + 1) * up_step)
        act_ref[:, cut] = jax.nn.gelu(dot(x, up_ref[:, cut], NN)).astype(BF16)
        share = asked // len(ups)
        mark_targets(rel, k * share, share, target_ref)
    kept = jnp.sum((ids_ref[...] != 0).astype(F32), axis=1, keepdims=True)
    place = lax.broadcasted_iota(jnp.int32, (length, 1), 0).astype(F32)
    down_copy.wait()
    rows = []
    for k in range(count):
        ffn = dot(act_ref[k * length : (k + 1) * length, :], down_ref[...], NN)
        centered, scale = normed(x_ref[k].astype(F32) + ffn)
        own = kept[k : k + 1, :]
        scale = jnp.where(place < own, scale, 0.0)
        rows.append(jnp.sum(centered * scale, axis=0, keepdims=True) / own)
    centered, scale = normed(jnp.concatenate(rows, axis=0))
    q_ref[...] = (centered * scale).astype(BF16)


def encode(states, ids, up_weight, down_weight, positives, counts, order, c_dev):
    count, length, width = states.shape
    hidden = up_weight.shape[1]
    asked, slots = positives.shape
    up_step = min(512, hidden)
    tokens = count * length
    return pl.pallas_call(
        functools.partial(encode_kernel, order, c_dev, up_step),
        out_shape=(pltpu.VMEM((count, width), BF16), pltpu.VMEM((asked, c_dev), F32)),
        in_specs=[pl.BlockSpec(memory_space=HBM)] * 6,
        out_specs=held(2),
        scratch_shapes=[
            pltpu.VMEM(states.shape, BF16),
            pltpu.VMEM(ids.shape, jnp.int32),
            pltpu.VMEM(up_weight.shape, BF16),
            pltpu.VMEM(down_weight.shape, BF16),
            pltpu.VMEM((slots, asked), jnp.int32),
            pltpu.VMEM((1, asked), jnp.int32),
            pltpu.VMEM((len(order), asked // len(order), slots), jnp.int32),
            pltpu.VMEM((tokens, hidden), BF16),
            pltpu.SemaphoreType.DMA((2, max(5, hidden // up_step))),
        ],
        compiler_params=pltpu.CompilerParams(vmem_limit_bytes=32 << 20),
        cost_estimate=pl.CostEstimate(
            flops=4 * tokens * hidden * width,
            transcendentals=tokens * hidden,
            bytes_accessed=4 * hidden * width + 2 * tokens * width,
        ),
        name="encode",
    )(*map(far, (states, ids, up_weight, down_weight, positives.T, counts.reshape(1, asked))))


def flip_kernel(first, src_ref, _, flip_ref, mark_ref):
    mark_ref[...] = jnp.zeros_like(mark_ref)
    rows = flip_ref.shape[1]
    sub = min(256, rows)
    for k in range(0, rows, sub):
        flip_ref[:, k : k + sub] = src_ref[first + k : first + k + sub, :].T


def flip(values, first, rows, behind):
    width = values.shape[1]
    return pl.pallas_call(
        functools.partial(flip_kernel, first),
        out_shape=(pltpu.VMEM((width, rows), values.dtype), pltpu.VMEM((8, 128), F32)),
        in_specs=held(2),
        out_specs=held(2),
        compiler_params=pltpu.CompilerParams(vmem_limit_bytes=4 << 20),
        cost_estimate=pl.CostEstimate(flops=0, transcendentals=0, bytes_accessed=2 * rows * width),
        name="flip",
    )(values, behind)


def join_kernel(a_ref, b_ref, *rest):
    out_ref = rest[-1]
    rows = a_ref.shape[0]
    out_ref[:rows, :] = a_ref[...]
    out_ref[rows:, :] = b_ref[...]


def join(a, b, *behind):
    rows, width = a.shape
    return pl.pallas_call(
        join_kernel,
        out_shape=pltpu.VMEM((2 * rows, width), a.dtype),
        in_specs=held(2 + len(behind)),
        out_specs=pl.BlockSpec(memory_space=pltpu.VMEM),
        compiler_params=pltpu.CompilerParams(vmem_limit_bytes=4 << 20),
        cost_estimate=pl.CostEstimate(flops=0, transcendentals=0, bytes_accessed=1024),
        name="join",
    )(a, b, *behind)


def outer_copies(first, rows, dlogit_ref, queries, out_hbm, held_ref, sems):
    copies = []
    for k in range(rows // 128):
        cut = slice(k * 128, (k + 1) * 128)
        held_ref[cut, :] = dot(dlogit_ref[:, first + k * 128 : first + (k + 1) * 128], queries, TN)
        copies.append(
            pltpu.make_async_copy(held_ref.at[cut], out_hbm.at[pl.ds(first + k * 128, 128)], sems.at[k])
        )
        copies[-1].start()
    return copies


def score_kernel(parts, qa_ref, qb_ref, target_ref, c_ref, *refs):
    flip_refs, (q_ref, keep_ref, send_ref, dlogit_ref, out_hbm, held_ref, sems) = refs[:parts], refs[parts:]
    half = qa_ref.shape[0]
    q_ref[:half, :] = qa_ref[...]
    q_ref[half:, :] = qb_ref[...]
    queries = q_ref[...]
    first = 0
    for flip_ref in flip_refs:
        columns = flip_ref.shape[1]
        for k in range(0, columns, 512):
            step = min(512, columns - k)
            logits = dot(queries, flip_ref[:, k : k + step], NN)
            cut = slice(first, first + step)
            dlogit_ref[:, cut] = (jax.nn.sigmoid(logits) * (1.0 / MB) - target_ref[:, cut]).astype(BF16)
            first += step
    copies = outer_copies(0, held_ref.shape[0], dlogit_ref, queries, out_hbm, held_ref, sems)
    grad = dot(dlogit_ref[...], c_ref[...], NN)
    keep_ref[...] = grad[:half]
    send_ref[...] = grad[half:]
    for copy in copies:
        copy.wait()


def score(centroids, flipped, qa, qb, target, rows):
    half, width = qa.shape
    count, c_dev = target.shape
    return pl.pallas_call(
        functools.partial(score_kernel, len(flipped)),
        out_shape=(
            pltpu.VMEM((count, width), BF16),
            pltpu.VMEM((half, width), F32),
            pltpu.VMEM((half, width), F32),
            pltpu.VMEM((count, c_dev), BF16),
            jax.ShapeDtypeStruct((c_dev, width), F32),
        ),
        in_specs=held(4 + len(flipped)),
        out_specs=(*held(4), pl.BlockSpec(memory_space=HBM)),
        scratch_shapes=[pltpu.VMEM((rows, width), F32), pltpu.SemaphoreType.DMA((rows // 128,))],
        compiler_params=pltpu.CompilerParams(vmem_limit_bytes=32 << 20),
        cost_estimate=pl.CostEstimate(
            flops=4 * count * c_dev * width, transcendentals=count * c_dev, bytes_accessed=2 * c_dev * width
        ),
        name="score",
    )(qa, qb, target, centroids, *flipped)


def outer_kernel(first, rows, dlogit_ref, q_ref, _, out_hbm, held_ref, sems):
    for copy in outer_copies(first, rows, dlogit_ref, q_ref[...], out_hbm, held_ref, sems):
        copy.wait()


def outer(dlogit, queries, first, rows, grown):
    count, c_dev = dlogit.shape
    width = queries.shape[1]
    return pl.pallas_call(
        functools.partial(outer_kernel, first, rows),
        out_shape=jax.ShapeDtypeStruct((c_dev, width), F32),
        in_specs=[*held(2), pl.BlockSpec(memory_space=HBM)],
        out_specs=pl.BlockSpec(memory_space=HBM),
        scratch_shapes=[pltpu.VMEM((rows, width), F32), pltpu.SemaphoreType.DMA((rows // 128,))],
        input_output_aliases={2: 0},
        compiler_params=pltpu.CompilerParams(vmem_limit_bytes=16 << 20),
        cost_estimate=pl.CostEstimate(
            flops=2 * count * rows * width, transcendentals=0, bytes_accessed=4 * rows * width
        ),
        name="outer",
    )(dlogit, queries, grown)


def shards(n, hidden_states, token_ids, up_weight, down_weight, centroids, positives, counts):
    bits = n.bit_length() - 1
    pairs = [1] + [1 << k | 1 for k in range(1, bits)]
    order = [0]
    for pair in reversed(pairs):
        order += [k ^ pair for k in order]
    c_dev = centroids.shape[0]

    def swap(values, pair):
        return lax.ppermute(values, "cluster", [(i, i ^ pair) for i in range(n)])

    queries, target = encode(
        hidden_states, token_ids, up_weight, down_weight, positives, counts, order, c_dev
    )
    cuts = [round(c_dev // 256 * share) * 256 for share in FETCH]
    flipped = []
    for k, pair in enumerate(reversed(pairs)):
        got = swap(queries, pair)
        marks = []
        if k < len(cuts) - 1 and cuts[k + 1] > cuts[k]:
            part, mark = flip(centroids, cuts[k], cuts[k + 1] - cuts[k], queries)
            flipped.append(part)
            marks.append(mark)
        if k < bits - 1:
            queries = join(queries, got, *marks)
    ends = [round(c_dev // 128 * share) * 128 for share in SHARES]
    first = max(128, round(c_dev // 128 * FIRST) * 128)
    queries, keep, send, dlogit, grown = score(centroids, flipped, queries, got, target, first)
    for k, pair in enumerate(pairs):
        got = swap(send, pair)
        if k < len(ends) and ends[k] > first:
            grown = outer(dlogit, queries, first, ends[k] - first, grown)
            first = ends[k]
            got, grown = lax.optimization_barrier((got, grown))
        total = keep + got
        half = total.shape[0] // 2
        keep, send = total[:half], total[half:]
    return (total, grown)


def solution(mesh):
    placed = (
        P(("groups", "cluster"), None, None),
        P(("groups", "cluster"), None),
        P(),
        P(),
        P("cluster", None),
        P("groups", None),
        P("groups"),
    )
    return jax.shard_map(
        functools.partial(shards, mesh.shape["cluster"]),
        mesh=mesh,
        in_specs=placed,
        out_specs=(P(("groups", "cluster"), None), P(("groups", "cluster"), None)),
        check_vma=False,
    )
```

```python
import functools

import jax
import jax.numpy as jnp
from jax import lax
from jax.experimental import pallas as pl
from jax.experimental.pallas import tpu as pltpu
from jax.sharding import PartitionSpec as P

MB = 32
EPS = 1e-05
F32 = jnp.float32
BF16 = jnp.bfloat16
FETCH = (0.0, 0.3125, 0.6875, 1.0)
FIRST = 0.25
SHARES = (0.0, 0.5625, 0.78125, 1.0)
HBM = pltpu.MemorySpace.HBM
NN = (((1,), (0,)), ((), ()))
NT = (((1,), (1,)), ((), ()))
TN = (((0,), (0,)), ((), ()))


def dot(a, b, dims):
    return lax.dot_general(a, b, dims, preferred_element_type=F32)


def held(count):
    return (pl.BlockSpec(memory_space=pltpu.VMEM),) * count


def far(values):
    return pltpu.with_memory_space_constraint(values, HBM)


def normed(values):
    centered = values - jnp.mean(values, axis=-1, keepdims=True)
    spread = jnp.mean(centered * centered, axis=-1, keepdims=True)
    return centered, lax.rsqrt(spread + EPS)


def mark_targets(rel, first, asked, target_ref):
    slots = rel.shape[1]
    tiles = target_ref.shape[1] // 128
    entries, rows = 8 * slots, 8 * tiles
    sub = lax.broadcasted_iota(jnp.int32, (8, 1), 0)
    low_at = lax.broadcasted_iota(jnp.int32, (entries, 128), 1)
    row_at = lax.broadcasted_iota(jnp.int32, (entries, rows), 1)
    for q in range(first, first + asked, 8):
        own = [rel[q : q + 8, s : s + 1] for s in range(slots)]
        low = jnp.concatenate([lax.bitwise_and(r, 127) for r in own], axis=0)
        row = jnp.concatenate([lax.shift_right_arithmetic(r, 7) * 8 + sub for r in own], axis=0)
        lows = jnp.where(low_at == low, 1.0, 0.0).astype(BF16)
        rows_hit = jnp.where(row_at == row, 1.0, 0.0).astype(BF16)
        hits = dot(rows_hit, lows, TN)
        for t in range(tiles):
            target_ref[q : q + 8, t * 128 : (t + 1) * 128] = jnp.where(
                hits[t * 8 : (t + 1) * 8, :] > 0.5, 1.0 / MB, 0.0
            )


def encode_kernel(
    order, c_dev, up_step, x_hbm, ids_hbm, up_hbm, down_hbm, pos_hbm, cnt_hbm, q_ref, target_ref,
    x_ref, ids_ref, up_ref, down_ref, pos_ref, cnt_ref, own_ref, act_ref, sems,
):
    count, length, width = x_ref.shape
    hidden = up_ref.shape[1]
    slots, asked = pos_ref.shape
    me = lax.axis_index("cluster")
    small = [
        pltpu.make_async_copy(src, dst, sems.at[0, k])
        for k, (src, dst) in enumerate([(pos_hbm, pos_ref), (cnt_hbm, cnt_ref), (ids_hbm, ids_ref)])
    ]
    x_copy = pltpu.make_async_copy(x_hbm, x_ref, sems.at[0, 3])
    down_copy = pltpu.make_async_copy(down_hbm, down_ref, sems.at[0, 4])
    ups = []
    for k in range(hidden // up_step):
        cut = (slice(None), pl.ds(k * up_step, up_step))
        ups.append(pltpu.make_async_copy(up_hbm.at[cut], up_ref.at[cut], sems.at[1, k]))
    for copy in small + [x_copy] + ups + [down_copy]:
        copy.start()
    for copy in small:
        copy.wait()
    slot = lax.broadcasted_iota(jnp.int32, (slots, asked), 0)
    rel = jnp.where(slot < cnt_ref[...], pos_ref[...] - me * c_dev, -1).T
    per = own_ref.shape[1]
    for k in range(asked // per):
        own_ref[k] = rel[k * per : (k + 1) * per, :]
    rel = jnp.concatenate([own_ref[lax.bitwise_xor(me, k)] for k in order], axis=0)
    x_copy.wait()
    x = x_ref[...].reshape(count * length, width)
    for k, copy in enumerate(ups):
        copy.wait()
        cut = slice(k * up_step, (k + 1) * up_step)
        act_ref[:, cut] = jax.nn.gelu(dot(x, up_ref[:, cut], NN)).astype(BF16)
        share = asked // len(ups)
        mark_targets(rel, k * share, share, target_ref)
    kept = jnp.sum((ids_ref[...] != 0).astype(F32), axis=1, keepdims=True)
    place = lax.broadcasted_iota(jnp.int32, (length, 1), 0).astype(F32)
    down_copy.wait()
    rows = []
    ahead = dot(act_ref[:length, :], down_ref[...], NN)
    for k in range(count):
        ffn = ahead
        if k + 1 < count:
            ahead = dot(act_ref[(k + 1) * length : (k + 2) * length, :], down_ref[...], NN)
        centered, scale = normed(x_ref[k].astype(F32) + ffn)
        own = kept[k : k + 1, :]
        scale = jnp.where(place < own, scale, 0.0)
        rows.append(jnp.sum(centered * scale, axis=0, keepdims=True) / own)
    centered, scale = normed(jnp.concatenate(rows, axis=0))
    q_ref[...] = (centered * scale).astype(BF16)


def encode(states, ids, up_weight, down_weight, positives, counts, order, c_dev):
    count, length, width = states.shape
    hidden = up_weight.shape[1]
    asked, slots = positives.shape
    up_step = min(512, hidden)
    tokens = count * length
    return pl.pallas_call(
        functools.partial(encode_kernel, order, c_dev, up_step),
        out_shape=(pltpu.VMEM((count, width), BF16), pltpu.VMEM((asked, c_dev), F32)),
        in_specs=[pl.BlockSpec(memory_space=HBM)] * 6,
        out_specs=held(2),
        scratch_shapes=[
            pltpu.VMEM(states.shape, BF16),
            pltpu.VMEM(ids.shape, jnp.int32),
            pltpu.VMEM(up_weight.shape, BF16),
            pltpu.VMEM(down_weight.shape, BF16),
            pltpu.VMEM((slots, asked), jnp.int32),
            pltpu.VMEM((1, asked), jnp.int32),
            pltpu.VMEM((len(order), asked // len(order), slots), jnp.int32),
            pltpu.VMEM((tokens, hidden), BF16),
            pltpu.SemaphoreType.DMA((2, max(5, hidden // up_step))),
        ],
        compiler_params=pltpu.CompilerParams(vmem_limit_bytes=32 << 20),
        cost_estimate=pl.CostEstimate(
            flops=4 * tokens * hidden * width,
            transcendentals=tokens * hidden,
            bytes_accessed=4 * hidden * width + 2 * tokens * width,
        ),
        name="encode",
    )(*map(far, (states, ids, up_weight, down_weight, positives.T, counts.reshape(1, asked))))


def flip_kernel(first, src_ref, _, flip_ref, mark_ref):
    mark_ref[...] = jnp.zeros_like(mark_ref)
    rows = flip_ref.shape[1]
    sub = min(256, rows)
    for k in range(0, rows, sub):
        flip_ref[:, k : k + sub] = src_ref[first + k : first + k + sub, :].T


def flip(values, first, rows, behind):
    width = values.shape[1]
    return pl.pallas_call(
        functools.partial(flip_kernel, first),
        out_shape=(pltpu.VMEM((width, rows), values.dtype), pltpu.VMEM((8, 128), F32)),
        in_specs=held(2),
        out_specs=held(2),
        compiler_params=pltpu.CompilerParams(vmem_limit_bytes=4 << 20),
        cost_estimate=pl.CostEstimate(flops=0, transcendentals=0, bytes_accessed=2 * rows * width),
        name="flip",
    )(values, behind)


def join_kernel(a_ref, b_ref, *rest):
    out_ref = rest[-1]
    rows = a_ref.shape[0]
    out_ref[:rows, :] = a_ref[...]
    out_ref[rows:, :] = b_ref[...]


def join(a, b, *behind):
    rows, width = a.shape
    return pl.pallas_call(
        join_kernel,
        out_shape=pltpu.VMEM((2 * rows, width), a.dtype),
        in_specs=held(2 + len(behind)),
        out_specs=pl.BlockSpec(memory_space=pltpu.VMEM),
        compiler_params=pltpu.CompilerParams(vmem_limit_bytes=4 << 20),
        cost_estimate=pl.CostEstimate(flops=0, transcendentals=0, bytes_accessed=1024),
        name="join",
    )(a, b, *behind)


def outer_copies(first, rows, dlogit_ref, queries, out_hbm, held_ref, sems):
    copies = []
    for k in range(rows // 128):
        cut = slice(k * 128, (k + 1) * 128)
        held_ref[cut, :] = dot(dlogit_ref[:, first + k * 128 : first + (k + 1) * 128], queries, TN)
        copies.append(
            pltpu.make_async_copy(held_ref.at[cut], out_hbm.at[pl.ds(first + k * 128, 128)], sems.at[k])
        )
        copies[-1].start()
    return copies


def score_kernel(parts, qa_ref, qb_ref, target_ref, c_ref, *refs):
    flip_refs, (q_ref, keep_ref, send_ref, dlogit_ref, out_hbm, held_ref, sems) = refs[:parts], refs[parts:]
    half = qa_ref.shape[0]
    q_ref[:half, :] = qa_ref[...]
    q_ref[half:, :] = qb_ref[...]
    queries = q_ref[...]
    first = 0
    for flip_ref in flip_refs:
        columns = flip_ref.shape[1]
        for k in range(0, columns, 512):
            step = min(512, columns - k)
            logits = dot(queries, flip_ref[:, k : k + step], NN)
            cut = slice(first, first + step)
            dlogit_ref[:, cut] = (jax.nn.sigmoid(logits) * (1.0 / MB) - target_ref[:, cut]).astype(BF16)
            first += step
    copies = outer_copies(0, held_ref.shape[0], dlogit_ref, queries, out_hbm, held_ref, sems)
    grad = dot(dlogit_ref[...], c_ref[...], NN)
    keep_ref[...] = grad[:half]
    send_ref[...] = grad[half:]
    for copy in copies:
        copy.wait()


def score(centroids, flipped, qa, qb, target, rows):
    half, width = qa.shape
    count, c_dev = target.shape
    return pl.pallas_call(
        functools.partial(score_kernel, len(flipped)),
        out_shape=(
            pltpu.VMEM((count, width), BF16),
            pltpu.VMEM((half, width), F32),
            pltpu.VMEM((half, width), F32),
            pltpu.VMEM((count, c_dev), BF16),
            jax.ShapeDtypeStruct((c_dev, width), F32),
        ),
        in_specs=held(4 + len(flipped)),
        out_specs=(*held(4), pl.BlockSpec(memory_space=HBM)),
        scratch_shapes=[pltpu.VMEM((rows, width), F32), pltpu.SemaphoreType.DMA((rows // 128,))],
        compiler_params=pltpu.CompilerParams(vmem_limit_bytes=32 << 20),
        cost_estimate=pl.CostEstimate(
            flops=4 * count * c_dev * width, transcendentals=count * c_dev, bytes_accessed=2 * c_dev * width
        ),
        name="score",
    )(qa, qb, target, centroids, *flipped)


def outer_kernel(first, rows, dlogit_ref, q_ref, _, out_hbm, held_ref, sems):
    for copy in outer_copies(first, rows, dlogit_ref, q_ref[...], out_hbm, held_ref, sems):
        copy.wait()


def outer(dlogit, queries, first, rows, grown):
    count, c_dev = dlogit.shape
    width = queries.shape[1]
    return pl.pallas_call(
        functools.partial(outer_kernel, first, rows),
        out_shape=jax.ShapeDtypeStruct((c_dev, width), F32),
        in_specs=[*held(2), pl.BlockSpec(memory_space=HBM)],
        out_specs=pl.BlockSpec(memory_space=HBM),
        scratch_shapes=[pltpu.VMEM((rows, width), F32), pltpu.SemaphoreType.DMA((rows // 128,))],
        input_output_aliases={2: 0},
        compiler_params=pltpu.CompilerParams(vmem_limit_bytes=16 << 20),
        cost_estimate=pl.CostEstimate(
            flops=2 * count * rows * width, transcendentals=0, bytes_accessed=4 * rows * width
        ),
        name="outer",
    )(dlogit, queries, grown)


def shards(n, hidden_states, token_ids, up_weight, down_weight, centroids, positives, counts):
    bits = n.bit_length() - 1
    pairs = [1] + [1 << k | 1 for k in range(1, bits)]
    order = [0]
    for pair in reversed(pairs):
        order += [k ^ pair for k in order]
    c_dev = centroids.shape[0]

    def swap(values, pair):
        return lax.ppermute(values, "cluster", [(i, i ^ pair) for i in range(n)])

    queries, target = encode(
        hidden_states, token_ids, up_weight, down_weight, positives, counts, order, c_dev
    )
    cuts = [round(c_dev // 256 * share) * 256 for share in FETCH]
    flipped = []
    for k, pair in enumerate(reversed(pairs)):
        got = swap(queries, pair)
        marks = []
        if k < len(cuts) - 1 and cuts[k + 1] > cuts[k]:
            part, mark = flip(centroids, cuts[k], cuts[k + 1] - cuts[k], queries)
            flipped.append(part)
            marks.append(mark)
        if k < bits - 1:
            queries = join(queries, got, *marks)
    ends = [round(c_dev // 128 * share) * 128 for share in SHARES]
    first = max(128, round(c_dev // 128 * FIRST) * 128)
    queries, keep, send, dlogit, grown = score(centroids, flipped, queries, got, target, first)
    for k, pair in enumerate(pairs):
        got = swap(send, pair)
        if k < len(ends) and ends[k] > first:
            grown = outer(dlogit, queries, first, ends[k] - first, grown)
            first = ends[k]
            got, grown = lax.optimization_barrier((got, grown))
        total = keep + got
        half = total.shape[0] // 2
        keep, send = total[:half], total[half:]
    return (total, grown)


def solution(mesh):
    placed = (
        P(("groups", "cluster"), None, None),
        P(("groups", "cluster"), None),
        P(),
        P(),
        P("cluster", None),
        P("groups", None),
        P("groups"),
    )
    return jax.shard_map(
        functools.partial(shards, mesh.shape["cluster"]),
        mesh=mesh,
        in_specs=placed,
        out_specs=(P(("groups", "cluster"), None), P(("groups", "cluster"), None)),
        check_vma=False,
    )
```
